32 devices in a mesh: dp: 16 (over z, y, x), tensor: 2 (over core).
Axes of the slice: x: 2, y: 2, z: 4, core: 2. Of those that a mesh axis runs over, the one named last changes fastest.
Arguments:
- image_tokens: bfloat16 [16, 256, 1536], P('dp'), may hold values from -6 to 6
- text_tokens: bfloat16 [16, 154, 1536], P('dp'), may hold values from -6 to 6
- image_cotangent: bfloat16 [16, 256, 1536], P('dp'), may hold values from -6 to 6
- text_cotangent: bfloat16 [16, 154, 1536], P('dp'), may hold values from -6 to 6
- timesteps: int32 [16], replicated, may hold values from 0 to 999
- mod_weight: float32 [2, 1536, 9216], P(None, None, ('dp', 'tensor')), may hold values from -0.15625 to 0.15625
- mod_bias: float32 [2, 9216], P(None, ('dp', 'tensor')), may hold values from -0.5 to 0.5
- qkv_weight: float32 [2, 1536, 3, 1536], P(None, 'dp', None, 'tensor'), may hold values from -1.2247449 to 1.2247449
- proj_weight: float32 [2, 1536, 1536], P(None, 'tensor', 'dp'), may hold values from -0.625 to 0.625
- up_weight: float32 [2, 1536, 6144], P(None, 'dp', 'tensor'), may hold values from -0.15625 to 0.15625
- down_weight: float32 [2, 6144, 1536], P(None, 'tensor', 'dp'), may hold values from -0.078125 to 0.078125
- mean_mod: float32 [2, 1536, 9216], P(None, None, ('dp', 'tensor')), may hold values from -3 to 3
- second_mod: float32 [2, 1536, 9216], P(None, None, ('dp', 'tensor')), may hold values from 0.01 to 0.5
- mean_bias: float32 [2, 9216], P(None, ('dp', 'tensor')), may hold values from -3 to 3
- second_bias: float32 [2, 9216], P(None, ('dp', 'tensor')), may hold values from 0.01 to 0.5
- mean_qkv: float32 [2, 1536, 3, 1536], P(None, 'dp', None, 'tensor'), may hold values from -3 to 3
- second_qkv: float32 [2, 1536, 3, 1536], P(None, 'dp', None, 'tensor'), may hold values from 0.01 to 0.5
- mean_proj: float32 [2, 1536, 1536], P(None, 'tensor', 'dp'), may hold values from -3 to 3
- second_proj: float32 [2, 1536, 1536], P(None, 'tensor', 'dp'), may hold values from 0.01 to 0.5
- mean_up: float32 [2, 1536, 6144], P(None, 'dp', 'tensor'), may hold values from -3 to 3
- second_up: float32 [2, 1536, 6144], P(None, 'dp', 'tensor'), may hold values from 0.01 to 0.5
- mean_down: float32 [2, 6144, 1536], P(None, 'tensor', 'dp'), may hold values from -3 to 3
- second_down: float32 [2, 6144, 1536], P(None, 'tensor', 'dp'), may hold values from 0.01 to 0.5
Outputs:
- image_out: float32 [16, 256, 1536], P('dp')
- text_out: float32 [16, 154, 1536], P('dp')
- image_grad: float32 [16, 256, 1536], P('dp')
- text_grad: float32 [16, 154, 1536], P('dp')
- grad_mod: float32 [2, 1536, 9216], P(None, None, ('dp', 'tensor'))
- grad_bias: float32 [2, 9216], P(None, ('dp', 'tensor'))
- grad_qkv: float32 [2, 1536, 3, 1536], P(None, 'dp', None, 'tensor')
- grad_proj: float32 [2, 1536, 1536], P(None, 'tensor', 'dp')
- grad_up: float32 [2, 1536, 6144], P(None, 'dp', 'tensor')
- grad_down: float32 [2, 6144, 1536], P(None, 'tensor', 'dp')
- new_mod: float32 [2, 1536, 9216], P(None, None, ('dp', 'tensor'))
- new_bias: float32 [2, 9216], P(None, ('dp', 'tensor'))
- new_qkv: float32 [2, 1536, 3, 1536], P(None, 'dp', None, 'tensor')
- new_proj: float32 [2, 1536, 1536], P(None, 'tensor', 'dp')
- new_up: float32 [2, 1536, 6144], P(None, 'dp', 'tensor')
- new_down: float32 [2, 6144, 1536], P(None, 'tensor', 'dp')
- mean_mod_next: float32 [2, 1536, 9216], P(None, None, ('dp', 'tensor'))
- second_mod_next: float32 [2, 1536, 9216], P(None, None, ('dp', 'tensor'))
- mean_bias_next: float32 [2, 9216], P(None, ('dp', 'tensor'))
- second_bias_next: float32 [2, 9216], P(None, ('dp', 'tensor'))
- mean_qkv_next: float32 [2, 1536, 3, 1536], P(None, 'dp', None, 'tensor')
- second_qkv_next: float32 [2, 1536, 3, 1536], P(None, 'dp', None, 'tensor')
- mean_proj_next: float32 [2, 1536, 1536], P(None, 'tensor', 'dp')
- second_proj_next: float32 [2, 1536, 1536], P(None, 'tensor', 'dp')
- mean_up_next: float32 [2, 1536, 6144], P(None, 'dp', 'tensor')
- second_up_next: float32 [2, 1536, 6144], P(None, 'dp', 'tensor')
- mean_down_next: float32 [2, 6144, 1536], P(None, 'tensor', 'dp')
- second_down_next: float32 [2, 6144, 1536], P(None, 'tensor', 'dp')
The draws below stay inside these ranges and needn't reach their ends.
All inputs are finite; a program needn't handle non-finite values.
Results may differ from the reference program's by a relative error of at most 0.012.
Values may be sent and summed in bfloat16 or wider, within the bound.
No kernel may reach another device: no remote copies, remote signals or barrier semaphores. Data moves between devices by JAX's collectives and lax.ppermute only.
A program may use at most 384 MiB of HBM per device.

```python
import math
import jax
import jax.numpy as jnp
from jax import lax

D = 1536
HEADS = 24
HD = 64
FF = 6144
TXT = 154
IMG = 256
ADAM_STEP = 10
SEQS = 16


def draw_qkv_weight(key, part):
    sampled = jnp.clip(jax.random.normal(key, (2, D, 3, D), jnp.float32), -6.0, 6.0) / math.sqrt(D)
    return sampled


def set_ends(values, key, smallest, high):
    longest = values.shape.index(max(values.shape))
    spots = []
    for shift in (0, 1):
        where = [jax.random.randint(jax.random.fold_in(key, axis), (), 0, length) for axis, length in enumerate(values.shape)]
        where[longest] = (where[longest] + shift) % values.shape[longest]
        spots.append(tuple(where))
    return values.at[spots[0]].set(smallest).at[spots[1]].set(high)


def steps_of(own_key, shape, pieces, smallest, largest):
    loudness, own = 1.0, jax.random.fold_in(own_key, 6)
    for position, shards_of in pieces:
        heights = jnp.exp(jax.random.uniform(jax.random.fold_in(own, position), (shards_of,), jnp.float32, smallest / len(pieces), largest / len(pieces)))
        loudness = loudness * jnp.repeat(heights, shape[position] // shards_of).reshape([-1 if axis == position else 1 for axis in range(len(shape))])
    return loudness


def gaussian(own_key, extent, scale, limit, split=(), kind=jnp.bfloat16):
    drawn = scale * jax.random.normal(own_key, extent, jnp.float32)
    if split:
        drawn = drawn * steps_of(own_key, extent, split, -0.22, 0.18)
    return jnp.clip(drawn, -limit, limit).astype(kind)


def setup_inputs(seed: int = 0) -> dict:
    seeds = jax.random.split(jax.random.key(seed), 24)
    return {
        "image_tokens": gaussian(seeds[0], (SEQS, IMG, D), 1.0, 6.0, ((0, 16),)),
        "text_tokens": gaussian(seeds[1], (SEQS, TXT, D), 1.0, 6.0, ((0, 16),)),
        "image_cotangent": gaussian(seeds[2], (SEQS, IMG, D), 1.0, 6.0, ((0, 16),)),
        "text_cotangent": gaussian(seeds[3], (SEQS, TXT, D), 1.0, 6.0, ((0, 16),)),
        "timesteps": set_ends(jax.random.randint(seeds[4], (SEQS,), 0, 1000), jax.random.fold_in(seeds[4], 1), 0, 999).astype(jnp.int32),
        "mod_weight": gaussian(seeds[5], (2, D, 6 * D), D ** -0.5, 0.15625, ((2, 32),), jnp.float32),
        "mod_bias": gaussian(seeds[6], (2, 6 * D), 0.08, 0.5, ((1, 32),), jnp.float32),
        "qkv_weight": draw_qkv_weight(jax.random.fold_in(seeds[23], 71), 0),
        "proj_weight": gaussian(seeds[8], (2, D, D), (max(1, D // 16)) ** -0.5, 0.625, ((1, 2), (2, 16)), jnp.float32),
        "up_weight": gaussian(seeds[9], (2, D, FF), D ** -0.5, 0.15625, ((1, 16), (2, 2)), jnp.float32),
        "down_weight": gaussian(seeds[10], (2, FF, D), FF ** -0.5, 0.078125, ((1, 2), (2, 16)), jnp.float32),
        "mean_mod": gaussian(seeds[11], (2, D, 6 * D), 0.5, 3.0, ((2, 32),), jnp.float32),
        "second_mod": jnp.clip(jnp.exp(math.log(0.5) - 3.912023 * jax.random.uniform(seeds[12], (2, D, 6 * D), jnp.float32) ** steps_of(seeds[12], (2, D, 6 * D), ((2, 32),), -0.2, 0.2)), 0.01, 0.5),
        "mean_bias": gaussian(seeds[13], (2, 6 * D), 0.5, 3.0, ((1, 32),), jnp.float32),
        "second_bias": jnp.clip(jnp.exp(math.log(0.5) - 3.912023 * jax.random.uniform(seeds[14], (2, 6 * D), jnp.float32) ** steps_of(seeds[14], (2, 6 * D), ((1, 32),), -0.2, 0.2)), 0.01, 0.5),
        "mean_qkv": gaussian(seeds[15], (2, D, 3, D), 0.5, 3.0, ((1, 16), (3, 2)), jnp.float32),
        "second_qkv": jnp.clip(jnp.exp(math.log(0.5) - 3.912023 * jax.random.uniform(seeds[16], (2, D, 3, D), jnp.float32) ** steps_of(seeds[16], (2, D, 3, D), ((1, 16), (3, 2)), -0.2, 0.2)), 0.01, 0.5),
        "mean_proj": gaussian(seeds[17], (2, D, D), 0.5, 3.0, ((1, 2), (2, 16)), jnp.float32),
        "second_proj": jnp.clip(jnp.exp(math.log(0.5) - 3.912023 * jax.random.uniform(seeds[18], (2, D, D), jnp.float32) ** steps_of(seeds[18], (2, D, D), ((1, 2), (2, 16)), -0.2, 0.2)), 0.01, 0.5),
        "mean_up": gaussian(seeds[19], (2, D, FF), 0.5, 3.0, ((1, 16), (2, 2)), jnp.float32),
        "second_up": jnp.clip(jnp.exp(math.log(0.5) - 3.912023 * jax.random.uniform(seeds[20], (2, D, FF), jnp.float32) ** steps_of(seeds[20], (2, D, FF), ((1, 16), (2, 2)), -0.2, 0.2)), 0.01, 0.5),
        "mean_down": gaussian(seeds[21], (2, FF, D), 0.5, 3.0, ((1, 2), (2, 16)), jnp.float32),
        "second_down": jnp.clip(jnp.exp(math.log(0.5) - 3.912023 * jax.random.uniform(seeds[22], (2, FF, D), jnp.float32) ** steps_of(seeds[22], (2, FF, D), ((1, 2), (2, 16)), -0.2, 0.2)), 0.01, 0.5),
    }


eps_norm = 1e-06
beta_one = 0.9
beta_two = 0.999
adam_eps = 1e-08
learn_rate = 0.02
decay_rate = 0.1
gelu_coef = 0.7978845608028654
cubic_coef = 0.044715

def rounded(values):
    return lax.optimization_barrier(values.astype(jnp.bfloat16)).astype(jnp.float32)

def layer_norm(values):
    average = lax.optimization_barrier(jnp.mean(values, axis=-1, keepdims=True))
    centred = values - average
    variance = lax.optimization_barrier(jnp.mean(centred * centred, axis=-1, keepdims=True))
    inv_std = lax.rsqrt(variance + eps_norm)
    return (centred * inv_std, inv_std)

def norm_back(grad_normed, normed, inv_std):
    mean_grad = lax.optimization_barrier(jnp.mean(grad_normed, axis=-1, keepdims=True))
    mean_cross = lax.optimization_barrier(jnp.mean(grad_normed * normed, axis=-1, keepdims=True))
    return inv_std * (grad_normed - mean_grad - normed * mean_cross)

def gelu_pair(inputs):
    argument = gelu_coef * (inputs + cubic_coef * inputs * inputs * inputs)
    tangent = jnp.tanh(argument)
    activated = 0.5 * inputs * (1.0 + tangent)
    derivative = 0.5 * (1.0 + tangent) + 0.5 * inputs * (1.0 - tangent * tangent) * gelu_coef * (1.0 + 3.0 * cubic_coef * inputs * inputs)
    return (activated, derivative)

def adam_step(weight, gradient, mean_old, second_old):
    mean_new = beta_one * mean_old + (1.0 - beta_one) * gradient
    second_new = beta_two * second_old + (1.0 - beta_two) * gradient * gradient
    mean_hat = mean_new / (1.0 - beta_one ** ADAM_STEP)
    second_hat = second_new / (1.0 - beta_two ** ADAM_STEP)
    updated = weight - learn_rate * (mean_hat / (jnp.sqrt(second_hat) + adam_eps) + decay_rate * weight)
    return (updated, mean_new, second_new)

def reference(image_tokens, text_tokens, image_cotangent, text_cotangent, timesteps, mod_weight, mod_bias, qkv_weight, proj_weight, up_weight, down_weight, mean_mod, second_mod, mean_bias, second_bias, mean_qkv, second_qkv, mean_proj, second_proj, mean_up, second_up, mean_down, second_down):
    length = IMG + TXT
    group_size = 2 if HEADS % 2 == 0 else 1
    score_scale = 1.0 / math.sqrt(HD)
    half_width = D // 2
    frequency = jnp.exp(-math.log(10000.0) * jnp.arange(half_width, dtype=jnp.float32) / half_width)
    angles = timesteps.astype(jnp.float32)[:, None] * frequency[None, :]
    cond = rounded(jax.nn.silu(jnp.concatenate([jnp.cos(angles), jnp.sin(angles)], axis=1)))
    mods_all = jnp.einsum('sd,ndc->snc', cond, rounded(mod_weight)) + rounded(mod_bias)[None, :, :]
    mods_all = mods_all.reshape(SEQS, 2, 6, D)
    qkv_low = rounded(qkv_weight)
    proj_low = rounded(proj_weight)
    up_low = rounded(up_weight)
    down_low = rounded(down_weight)

    def to_groups(row_block):
        per_head = row_block.reshape(length, HEADS, HD).transpose(1, 0, 2)
        return per_head.reshape(HEADS // group_size, group_size, length, HD)

    def from_groups(groups):
        return groups.reshape(HEADS, length, HD).transpose(1, 0, 2).reshape(length, D)

    def attend_forward(operands):
        queries, key_rows, value_rows = operands
        scores = jnp.einsum('gqd,gkd->gqk', queries, key_rows) * score_scale
        highest = lax.optimization_barrier(jnp.max(scores, axis=-1, keepdims=True))
        weights = jnp.exp(scores - highest)
        totals = lax.optimization_barrier(jnp.sum(weights, axis=-1, keepdims=True))
        probs_low = rounded(weights / totals)
        context = rounded(jnp.einsum('gqk,gkd->gqd', probs_low, value_rows))
        return (context, highest[..., 0] + jnp.log(totals[..., 0]))

    def attend_backward(operands):
        queries, key_rows, value_rows, context, logsumexp, grad_context = operands
        scores = jnp.einsum('gqd,gkd->gqk', queries, key_rows) * score_scale
        probs_full = jnp.exp(scores - logsumexp[..., None])
        grad_values = jnp.einsum('gqk,gqd->gkd', rounded(probs_full), grad_context)
        grad_probs = jnp.einsum('gqd,gkd->gqk', grad_context, value_rows)
        row_dots = lax.optimization_barrier(jnp.sum(grad_context * context, axis=-1, keepdims=True))
        grad_scores = rounded(probs_full * (grad_probs - row_dots) * score_scale)
        grad_queries = jnp.einsum('gqk,gkd->gqd', grad_scores, key_rows)
        grad_keys = jnp.einsum('gqk,gqd->gkd', grad_scores, queries)
        return (grad_queries, grad_keys, grad_values)

    def one_sequence(carry, operands):
        image_in, text_in, image_cot, text_cot, mods = operands
        inputs = (image_in.astype(jnp.float32), text_in.astype(jnp.float32))
        cotangents = (image_cot.astype(jnp.float32), text_cot.astype(jnp.float32))
        normed_one, inv_one, shifted_one, qkv_rows = ([], [], [], [])
        for stream in range(2):
            normed, inv_std = layer_norm(inputs[stream])
            shifted = rounded(normed * (1.0 + mods[stream, 1]) + mods[stream, 0])
            qkv_rows.append(rounded(jnp.einsum('td,dkc->tkc', shifted, qkv_low[stream])))
            normed_one.append(normed)
            inv_one.append(inv_std)
            shifted_one.append(shifted)
        joint = jnp.concatenate(qkv_rows, axis=0)
        query_groups = to_groups(joint[:, 0])
        key_groups = to_groups(joint[:, 1])
        value_groups = to_groups(joint[:, 2])
        context_groups, logsumexp = lax.map(attend_forward, (query_groups, key_groups, value_groups))
        context = from_groups(context_groups)
        contexts = (context[:IMG], context[IMG:])
        attn_sums, middles, normed_two, inv_two, shifted_two, derivs, hiddens, down_sums, outputs = ([], [], [], [], [], [], [], [], [])
        for stream in range(2):
            attn = jnp.dot(contexts[stream], proj_low[stream])
            middle = inputs[stream] + mods[stream, 2] * attn
            normed, inv_std = layer_norm(middle)
            shifted = rounded(normed * (1.0 + mods[stream, 4]) + mods[stream, 3])
            activated, derivative = gelu_pair(jnp.dot(shifted, up_low[stream]))
            hidden = rounded(activated)
            down = jnp.dot(hidden, down_low[stream])
            outputs.append(middle + mods[stream, 5] * down)
            attn_sums.append(attn)
            middles.append(middle)
            normed_two.append(normed)
            inv_two.append(inv_std)
            shifted_two.append(shifted)
            derivs.append(derivative)
            hiddens.append(hidden)
            down_sums.append(down)
        grad_down_list, grad_up_list, grad_proj_list, grad_context_list, grad_middles, partial_rows = ([], [], [], [], [], [])
        for stream in range(2):
            cotangent = cotangents[stream]
            grad_gate_two = lax.optimization_barrier(jnp.sum(cotangent * down_sums[stream], axis=0))
            grad_down_in = rounded(cotangent * mods[stream, 5])
            grad_down_list.append(jnp.dot(hiddens[stream].T, grad_down_in))
            grad_pre = rounded(jnp.dot(grad_down_in, down_low[stream].T) * derivs[stream])
            grad_up_list.append(jnp.dot(shifted_two[stream].T, grad_pre))
            grad_shifted = jnp.dot(grad_pre, up_low[stream].T)
            grad_shift_two = lax.optimization_barrier(jnp.sum(grad_shifted, axis=0))
            grad_scale_two = lax.optimization_barrier(jnp.sum(grad_shifted * normed_two[stream], axis=0))
            grad_middle = cotangent + norm_back(grad_shifted * (1.0 + mods[stream, 4]), normed_two[stream], inv_two[stream])
            grad_gate_one = lax.optimization_barrier(jnp.sum(grad_middle * attn_sums[stream], axis=0))
            grad_proj_in = rounded(grad_middle * mods[stream, 2])
            grad_proj_list.append(jnp.dot(contexts[stream].T, grad_proj_in))
            grad_context_list.append(rounded(jnp.dot(grad_proj_in, proj_low[stream].T)))
            grad_middles.append(grad_middle)
            partial_rows.append((grad_gate_one, grad_shift_two, grad_scale_two, grad_gate_two))
        grad_context_groups = to_groups(jnp.concatenate(grad_context_list, axis=0))
        grad_q, grad_k, grad_v = lax.map(attend_backward, (query_groups, key_groups, value_groups, context_groups, logsumexp, grad_context_groups))
        grad_joint = rounded(jnp.stack([from_groups(grad_q), from_groups(grad_k), from_groups(grad_v)], axis=1))
        grad_joint_rows = (grad_joint[:IMG], grad_joint[IMG:])
        grad_qkv_list, input_grads, mod_rows = ([], [], [])
        for stream in range(2):
            grad_qkv_list.append(jnp.einsum('td,tkc->dkc', shifted_one[stream], grad_joint_rows[stream]))
            grad_shifted = jnp.einsum('tkc,dkc->td', grad_joint_rows[stream], qkv_low[stream])
            grad_shift_one = lax.optimization_barrier(jnp.sum(grad_shifted, axis=0))
            grad_scale_one = lax.optimization_barrier(jnp.sum(grad_shifted * normed_one[stream], axis=0))
            input_grads.append(grad_middles[stream] + norm_back(grad_shifted * (1.0 + mods[stream, 1]), normed_one[stream], inv_one[stream]))
            grad_gate_one, grad_shift_two, grad_scale_two, grad_gate_two = partial_rows[stream]
            mod_rows.append(jnp.stack([grad_shift_one, grad_scale_one, grad_gate_one, grad_shift_two, grad_scale_two, grad_gate_two]))
        new_carry = (carry[0] + jnp.stack(grad_qkv_list), carry[1] + jnp.stack(grad_proj_list), carry[2] + jnp.stack(grad_up_list), carry[3] + jnp.stack(grad_down_list))
        return (new_carry, (outputs[0], outputs[1], input_grads[0], input_grads[1], jnp.stack(mod_rows)))
    start = (jnp.zeros((2, D, 3, D), jnp.float32), jnp.zeros((2, D, D), jnp.float32), jnp.zeros((2, D, FF), jnp.float32), jnp.zeros((2, FF, D), jnp.float32))
    sums, stacked = lax.scan(one_sequence, start, (image_tokens, text_tokens, image_cotangent, text_cotangent, mods_all))
    grad_qkv, grad_proj, grad_up, grad_down = sums
    image_out, text_out, image_grad, text_grad, mod_grad_rows = stacked
    mod_grad_rows = mod_grad_rows.reshape(SEQS, 2, 6 * D)
    grad_mod = jnp.einsum('sd,snc->ndc', cond, mod_grad_rows, precision=lax.Precision.HIGHEST)
    grad_bias = lax.optimization_barrier(jnp.sum(mod_grad_rows, axis=0))
    new_mod, mean_mod_next, second_mod_next = adam_step(mod_weight, grad_mod, mean_mod, second_mod)
    new_bias, mean_bias_next, second_bias_next = adam_step(mod_bias, grad_bias, mean_bias, second_bias)
    new_qkv, mean_qkv_next, second_qkv_next = adam_step(qkv_weight, grad_qkv, mean_qkv, second_qkv)
    new_proj, mean_proj_next, second_proj_next = adam_step(proj_weight, grad_proj, mean_proj, second_proj)
    new_up, mean_up_next, second_up_next = adam_step(up_weight, grad_up, mean_up, second_up)
    new_down, mean_down_next, second_down_next = adam_step(down_weight, grad_down, mean_down, second_down)
    return (image_out, text_out, image_grad, text_grad, grad_mod, grad_bias, grad_qkv, grad_proj, grad_up, grad_down, new_mod, new_bias, new_qkv, new_proj, new_up, new_down, mean_mod_next, second_mod_next, mean_bias_next, second_bias_next, mean_qkv_next, second_qkv_next, mean_proj_next, second_proj_next, mean_up_next, second_up_next, mean_down_next, second_down_next)
```

```python
import functools
import math

import jax
import jax.numpy as jnp
from jax import lax
from jax.experimental import pallas as pl
from jax.experimental.pallas import tpu as pltpu
from jax.sharding import Mesh
from jax.sharding import PartitionSpec as P


HD = 64
ADAM_STEP = 10
INNER = 4

eps_norm = 1e-06
beta_one = 0.9
beta_two = 0.999
adam_eps = 1e-08
learn_rate = 0.02
decay_rate = 0.1
gelu_coef = 0.7978845608028654
cubic_coef = 0.044715
score_scale = 1.0 / math.sqrt(HD)
NEGATIVE = -1e30
LANES = 128

F32 = jnp.float32
BF16 = jnp.bfloat16


def layer_norm(values):
    average = jnp.mean(values, axis=-1, keepdims=True)
    centred = values - average
    variance = jnp.mean(centred * centred, axis=-1, keepdims=True)
    inv_std = lax.rsqrt(variance + eps_norm)
    return (centred * inv_std, inv_std)


def norm_back(grad_normed, normed, inv_std):
    mean_grad = jnp.mean(grad_normed, axis=-1, keepdims=True)
    mean_cross = jnp.mean(grad_normed * normed, axis=-1, keepdims=True)
    return inv_std * (grad_normed - mean_grad - normed * mean_cross)


def gelu_pair(inputs):
    argument = gelu_coef * (inputs + cubic_coef * inputs * inputs * inputs)
    tangent = jnp.tanh(argument)
    activated = 0.5 * inputs * (1.0 + tangent)
    derivative = 0.5 * (1.0 + tangent) + 0.5 * inputs * (1.0 - tangent * tangent) * gelu_coef * (
        1.0 + 3.0 * cubic_coef * inputs * inputs
    )
    return (activated, derivative)


def adam_step(weight, gradient, mean_old, second_old):
    mean_new = beta_one * mean_old + (1.0 - beta_one) * gradient
    second_new = beta_two * second_old + (1.0 - beta_two) * gradient * gradient
    mean_hat = mean_new / (1.0 - beta_one**ADAM_STEP)
    second_hat = second_new / (1.0 - beta_two**ADAM_STEP)
    updated = weight - learn_rate * (
        mean_hat / (jnp.sqrt(second_hat) + adam_eps) + decay_rate * weight
    )
    return (updated, mean_new, second_new)


def dot_nn(a, b):
    return lax.dot_general(a, b, (((1,), (0,)), ((), ())), preferred_element_type=F32)


def dot_nt(a, b):
    return lax.dot_general(a, b, (((1,), (1,)), ((), ())), preferred_element_type=F32)


def dot_tn(a, b):
    return lax.dot_general(a, b, (((0,), (0,)), ((), ())), preferred_element_type=F32)


def key_bias(valid_ref, rows, padded):
    image, text = rows
    column = lax.broadcasted_iota(jnp.int32, (1, padded), 1)
    first = 2 * image
    second = first + text
    real = (column < first + valid_ref[0]) | ((column >= second) & (column < second + valid_ref[1]))
    return jnp.where(real, 0.0, NEGATIVE)


def pieces_of(rows):
    image, text = rows
    return ((0, image), (image, image), (2 * image, text), (2 * image + text, text))


def attend_kernel(rows, heads, padded, valid_ref, *refs):
    qkv, contexts, lse_ref, joint = (refs[:4], refs[4:8], refs[8], refs[9])
    width = heads * HD
    pieces = pieces_of(rows)
    total = 2 * sum(rows)
    for ref, (offset, size) in zip(qkv, pieces):
        joint[offset : offset + size, :] = ref[:, : 3 * width]
    if padded > total:
        joint[total:, :] = jnp.zeros((padded - total, 3 * width), BF16)
    bias = key_bias(valid_ref, rows, padded)
    for head in range(heads):
        at = head * HD
        keys = joint[:, width + at : width + at + HD]
        values = joint[:, 2 * width + at : 2 * width + at + HD]
        for ref, out, (offset, size) in zip(qkv, contexts, pieces):
            scores = dot_nt(ref[:, at : at + HD], keys) * score_scale + bias
            highest = jnp.max(scores, axis=-1, keepdims=True)
            weights = jnp.exp(scores - highest)
            totals = jnp.sum(weights, axis=-1, keepdims=True)
            probs = (weights * (1.0 / totals)).astype(BF16)
            out[:, at : at + HD] = dot_nn(probs, values).astype(BF16)
            lse_ref[offset : offset + size, head : head + 1] = highest + jnp.log(totals)


def attend_back_kernel(rows, heads, padded, valid_ref, *refs):
    qkv, contexts, grads, lse_ref = (refs[:4], refs[4:8], refs[8:12], refs[12])
    outs, joint, key_sum, value_sum = (refs[13:17], refs[17], refs[18], refs[19])
    width = heads * HD
    pieces = pieces_of(rows)
    total = 2 * sum(rows)
    for ref, (offset, size) in zip(qkv, pieces):
        joint[offset : offset + size, :] = ref[:, : 3 * width]
    if padded > total:
        joint[total:, :] = jnp.zeros((padded - total, 3 * width), BF16)
    bias = key_bias(valid_ref, rows, padded)
    for head in range(heads):
        at = head * HD
        keys = joint[:, width + at : width + at + HD]
        values = joint[:, 2 * width + at : 2 * width + at + HD]
        for number, (offset, size) in enumerate(pieces):
            queries = qkv[number][:, at : at + HD]
            grad_context = grads[number][:, at : at + HD]
            context = contexts[number][:, at : at + HD]
            scores = dot_nt(queries, keys) * score_scale + bias
            probs = jnp.exp(scores - lse_ref[offset : offset + size, head : head + 1])
            grad_probs = dot_nt(grad_context, values)
            row_dots = jnp.sum(
                grad_context.astype(F32) * context.astype(F32), axis=-1, keepdims=True
            )
            grad_scores = (probs * (grad_probs - row_dots) * score_scale).astype(BF16)
            outs[number][:, at : at + HD] = dot_nn(grad_scores, keys).astype(BF16)
            value_part = dot_tn(probs.astype(BF16), grad_context)
            key_part = dot_tn(grad_scores, queries)
            if number == 0:
                value_sum[...] = value_part
                key_sum[...] = key_part
            else:
                value_sum[...] += value_part
                key_sum[...] += key_part
        for number, (offset, size) in enumerate(pieces):
            outs[number][:, width + at : width + at + HD] = key_sum[
                offset : offset + size, :
            ].astype(BF16)
            outs[number][:, 2 * width + at : 2 * width + at + HD] = value_sum[
                offset : offset + size, :
            ].astype(BF16)


def piece_specs(rows, columns):
    image, text = rows
    return [pl.BlockSpec((size, columns), lambda s, v: (s, 0)) for size in (image, image, text, text)]


def attend(rows, heads, seqs, valid, qkv):
    total = 2 * sum(rows)
    padded = -(-total // LANES) * LANES
    width = heads * HD
    sizes = (rows[0], rows[0], rows[1], rows[1])
    return pl.pallas_call(
        functools.partial(attend_kernel, rows, heads, padded),
        grid_spec=pltpu.PrefetchScalarGridSpec(
            num_scalar_prefetch=1,
            grid=(seqs,),
            in_specs=piece_specs(rows, qkv[0].shape[1]),
            out_specs=piece_specs(rows, width)
            + [pl.BlockSpec((None, total, LANES), lambda s, v: (s, 0, 0))],
            scratch_shapes=[pltpu.VMEM((padded, 3 * width), BF16)],
        ),
        out_shape=[jax.ShapeDtypeStruct((seqs * size, width), BF16) for size in sizes]
        + [jax.ShapeDtypeStruct((seqs, total, LANES), F32)],
        cost_estimate=pl.CostEstimate(
            flops=4 * seqs * heads * total * total * HD,
            bytes_accessed=8 * seqs * total * width,
            transcendentals=seqs * heads * total * total,
        ),
        name="attend",
    )(valid, *qkv)


def attend_back(rows, heads, seqs, valid, qkv, contexts, grads, lse):
    total = 2 * sum(rows)
    padded = -(-total // LANES) * LANES
    width = heads * HD
    sizes = (rows[0], rows[0], rows[1], rows[1])
    return pl.pallas_call(
        functools.partial(attend_back_kernel, rows, heads, padded),
        grid_spec=pltpu.PrefetchScalarGridSpec(
            num_scalar_prefetch=1,
            grid=(seqs,),
            in_specs=piece_specs(rows, qkv[0].shape[1])
            + piece_specs(rows, width)
            + piece_specs(rows, width)
            + [pl.BlockSpec((None, total, LANES), lambda s, v: (s, 0, 0))],
            out_specs=piece_specs(rows, 3 * width),
            scratch_shapes=[
                pltpu.VMEM((padded, 3 * width), BF16),
                pltpu.VMEM((padded, HD), F32),
                pltpu.VMEM((padded, HD), F32),
            ],
        ),
        out_shape=[jax.ShapeDtypeStruct((seqs * size, 3 * width), BF16) for size in sizes],
        cost_estimate=pl.CostEstimate(
            flops=10 * seqs * heads * total * total * HD,
            bytes_accessed=20 * seqs * total * width,
            transcendentals=seqs * heads * total * total,
        ),
        name="attend_back",
    )(valid, *qkv, *contexts, *grads, lse)


def swap_core(values):
    return lax.ppermute(values, "tensor", [(0, 1), (1, 0)])


def hop(values, distance, count):
    return lax.ppermute(values, "inner", [(i, i ^ distance) for i in range(count)])


def gather_rows(rows, count):
    own = jnp.concatenate([rows] + [hop(rows, j, count) for j in range(1, count)], axis=0)
    return (own, swap_core(own))


def sum_rows(own, other, count):
    arrived = swap_core(other.astype(BF16))
    blocks = (own + arrived.astype(F32)).reshape(count, own.shape[0] // count, own.shape[1])
    low = blocks.astype(BF16)
    total = blocks[0]
    for j in range(1, count):
        total = total + hop(low[j], j, count).astype(F32)
    return total


def by_number(blocks, me, count):
    stacked = jnp.stack(blocks)
    shape = stacked.shape
    bit = 1
    while bit < count:
        split = stacked.reshape((count // (2 * bit), 2, bit) + shape[1:])
        split = jnp.where((me & bit) != 0, split[:, ::-1], split)
        stacked = split.reshape(shape)
        bit *= 2
    return stacked


def exchange(block_of, me, count):
    blocks = [block_of(me)]
    for j in range(1, count):
        blocks.append(hop(block_of(me ^ j), j, count))
    return by_number(blocks, me, count)


def local(
    image_tokens,
    text_tokens,
    image_cotangent,
    text_cotangent,
    timesteps,
    mod_weight,
    mod_bias,
    qkv_weight,
    proj_weight,
    up_weight,
    down_weight,
    mean_mod,
    second_mod,
    mean_bias,
    second_bias,
    mean_qkv,
    second_qkv,
    mean_proj,
    second_proj,
    mean_up,
    second_up,
    mean_down,
    second_down,
):
    count = lax.axis_size("inner")
    cores = lax.axis_size("tensor")
    me = lax.axis_index("inner")
    core = lax.axis_index("tensor")
    every = ("outer", "inner", "tensor")
    streams = (0, 1)
    seq_count = timesteps.shape[0]
    devices = seq_count * cores
    column_count = mod_weight.shape[2]
    width = image_tokens.shape[2]
    slab = qkv_weight.shape[1]
    head_cols = qkv_weight.shape[3] // count
    heads = head_cols // HD
    unit_cols = up_weight.shape[2] // count
    lengths = (image_tokens.shape[1], text_tokens.shape[1])
    rows = tuple(-(-length // (16 * cores)) * 16 for length in lengths)

    half_width = width // 2
    frequency = jnp.exp(-math.log(10000.0) * jnp.arange(half_width, dtype=F32) / half_width)
    angles = timesteps.astype(F32)[:, None] * frequency[None, :]
    all_cond = jax.nn.silu(jnp.concatenate([jnp.cos(angles), jnp.sin(angles)], axis=1)).astype(BF16)
    bias_low = lax.optimization_barrier(mod_bias.astype(BF16)).astype(F32)
    local_mod = (
        jnp.einsum("sd,ndc->snc", all_cond, mod_weight.astype(BF16), preferred_element_type=F32)
        + bias_low[None, :, :]
    )
    to_cores = jnp.broadcast_to(
        local_mod[:, None], (seq_count, cores, 2, column_count)
    ).reshape(devices, 2, column_count)
    spread = lax.all_to_all(to_cores, every, split_axis=0, concat_axis=0, tiled=True)
    mods = spread.transpose(1, 0, 2).reshape(2, 6, width)

    qkv_low = qkv_weight.astype(BF16)
    proj_low = proj_weight.astype(BF16).transpose(0, 2, 1)
    up_low = up_weight.astype(BF16)
    down_low = down_weight.astype(BF16).transpose(0, 2, 1)

    def attn_block(n, i):
        part = lax.dynamic_slice(qkv_low[n], (0, 0, i * head_cols), (slab, 3, head_cols))
        tail = lax.dynamic_slice(proj_low[n], (0, i * head_cols), (slab, head_cols))
        return jnp.concatenate([part.reshape(slab, 3 * head_cols), tail], axis=1)

    def up_block(n, i):
        return lax.dynamic_slice(up_low[n], (0, i * unit_cols), (slab, unit_cols))

    def down_block(n, i):
        return lax.dynamic_slice(down_low[n], (0, i * unit_cols), (slab, unit_cols))

    def full_weight(block):
        shard = exchange(block, me, count)
        shard = shard.reshape(count * slab, shard.shape[2])
        return lax.all_gather(shard, "outer", axis=0, tiled=True)

    attn_full, up_full, down_full = ([], [], [])
    for block, full in ((attn_block, attn_full), (up_block, up_full), (down_block, down_full)):
        for n in streams:
            full.append(full_weight(functools.partial(block, n)))
    qkv_full = [full[:, : 3 * head_cols] for full in attn_full]
    proj_full = [full[:, 3 * head_cols :] for full in attn_full]

    def own_rows(tokens, size):
        short = cores * size - tokens.shape[1]
        padded = jnp.pad(tokens[0], ((0, short), (0, 0)))
        return lax.dynamic_slice(padded, (core * size, 0), (size, width))

    inputs = [own_rows(t, r).astype(F32) for t, r in zip((image_tokens, text_tokens), rows)]
    cotangents = [own_rows(t, r).astype(F32) for t, r in zip((image_cotangent, text_cotangent), rows)]
    valid = jnp.stack(
        [
            jnp.clip(lengths[1] - core * rows[1], 0, rows[1]),
            jnp.clip(lengths[1] - (1 - core) * rows[1], 0, rows[1]),
        ]
    ).astype(jnp.int32)

    normed_one, inv_one, shifted_one, qkv_rows = ([], [], [], [])
    for n in streams:
        normed, inv_std = layer_norm(inputs[n])
        shifted = (normed * (1.0 + mods[n, 1]) + mods[n, 0]).astype(BF16)
        halves = gather_rows(shifted, count)
        qkv_rows.append([dot_nn(half, qkv_full[n]).astype(BF16) for half in halves])
        normed_one.append(normed)
        inv_one.append(inv_std)
        shifted_one.append(halves)
    qkv_pieces = qkv_rows[0] + qkv_rows[1]
    *context_pieces, lse = attend(rows, heads, count, valid, qkv_pieces)
    contexts = (context_pieces[:2], context_pieces[2:])

    attn_sums, middles, normed_two, inv_two, shifted_two = ([], [], [], [], [])
    derivs, hiddens, down_sums, outputs = ([], [], [], [])
    for n in streams:
        partial = [dot_nt(half, proj_full[n]) for half in contexts[n]]
        attn_sum = sum_rows(partial[0], partial[1], count)
        middle = inputs[n] + mods[n, 2] * attn_sum
        normed, inv_std = layer_norm(middle)
        shifted = (normed * (1.0 + mods[n, 4]) + mods[n, 3]).astype(BF16)
        halves = gather_rows(shifted, count)
        pairs = [gelu_pair(dot_nn(half, up_full[n])) for half in halves]
        hidden = [pair[0].astype(BF16) for pair in pairs]
        partial = [dot_nt(half, down_full[n]) for half in hidden]
        down_sum = sum_rows(partial[0], partial[1], count)
        attn_sums.append(attn_sum)
        middles.append(middle)
        normed_two.append(normed)
        inv_two.append(inv_std)
        shifted_two.append(halves)
        derivs.append([pair[1] for pair in pairs])
        hiddens.append(hidden)
        down_sums.append(down_sum)
        outputs.append(middle + mods[n, 5] * down_sum)

    def owned(gradient):
        summed = lax.psum_scatter(gradient.astype(BF16), "outer", scatter_dimension=0, tiled=True)
        block = lambda i: lax.dynamic_slice(summed, (i * slab, 0), (slab, summed.shape[1]))
        return exchange(block, me, count).astype(F32)

    grad_down_list, grad_up_list, grad_attn_list = ([], [], [])
    grad_contexts, grad_middles, partial_rows, proj_ins = ([], [], [], [])
    for n in streams:
        cotangent = cotangents[n]
        grad_gate_two = jnp.sum(cotangent * down_sums[n], axis=0)
        down_ins = gather_rows((cotangent * mods[n, 5]).astype(BF16), count)
        grad_down_list.append(
            owned(dot_tn(down_ins[0], hiddens[n][0]) + dot_tn(down_ins[1], hiddens[n][1]))
        )
        grad_pres = [
            (dot_nn(down_in, down_full[n]) * deriv).astype(BF16)
            for down_in, deriv in zip(down_ins, derivs[n])
        ]
        grad_up_list.append(
            owned(dot_tn(shifted_two[n][0], grad_pres[0]) + dot_tn(shifted_two[n][1], grad_pres[1]))
        )
        partial = [dot_nt(grad_pre, up_full[n]) for grad_pre in grad_pres]
        grad_shifted = sum_rows(partial[0], partial[1], count)
        grad_shift_two = jnp.sum(grad_shifted, axis=0)
        grad_scale_two = jnp.sum(grad_shifted * normed_two[n], axis=0)
        grad_middle = cotangent + norm_back(
            grad_shifted * (1.0 + mods[n, 4]), normed_two[n], inv_two[n]
        )
        grad_gate_one = jnp.sum(grad_middle * attn_sums[n], axis=0)
        halves = gather_rows((grad_middle * mods[n, 2]).astype(BF16), count)
        grad_contexts += [dot_nn(half, proj_full[n]).astype(BF16) for half in halves]
        proj_ins.append(halves)
        grad_middles.append(grad_middle)
        partial_rows.append((grad_gate_one, grad_shift_two, grad_scale_two, grad_gate_two))
    grad_pieces = attend_back(
        rows, heads, count, valid, qkv_pieces, context_pieces, grad_contexts, lse
    )
    grad_qkv_rows = (grad_pieces[:2], grad_pieces[2:])
    input_grads, mod_rows = ([], [])
    for n in streams:
        grad_attn_list.append(
            owned(
                jnp.concatenate(
                    [
                        dot_tn(shifted_one[n][0], grad_qkv_rows[n][0])
                        + dot_tn(shifted_one[n][1], grad_qkv_rows[n][1]),
                        dot_tn(proj_ins[n][0], contexts[n][0])
                        + dot_tn(proj_ins[n][1], contexts[n][1]),
                    ],
                    axis=1,
                )
            )
        )
        partial = [dot_nt(half, qkv_full[n]) for half in grad_qkv_rows[n]]
        grad_shifted = sum_rows(partial[0], partial[1], count)
        grad_shift_one = jnp.sum(grad_shifted, axis=0)
        grad_scale_one = jnp.sum(grad_shifted * normed_one[n], axis=0)
        input_grads.append(
            grad_middles[n]
            + norm_back(grad_shifted * (1.0 + mods[n, 1]), normed_one[n], inv_one[n])
        )
        grad_gate_one, grad_shift_two, grad_scale_two, grad_gate_two = partial_rows[n]
        mod_rows.append(
            jnp.concatenate(
                [
                    grad_shift_one,
                    grad_scale_one,
                    grad_gate_one,
                    grad_shift_two,
                    grad_scale_two,
                    grad_gate_two,
                ]
            )
        )

    def whole_rows(own, length):
        other = swap_core(own)
        first = jnp.where(core == 0, own, other)
        second = jnp.where(core == 0, other, own)
        return jnp.concatenate([first, second], axis=0)[None, :length]

    image_out, text_out = (whole_rows(o, length) for o, length in zip(outputs, lengths))
    image_grad, text_grad = (whole_rows(g, length) for g, length in zip(input_grads, lengths))

    to_owners = jnp.stack(mod_rows).reshape(2, devices, column_count).transpose(1, 0, 2)
    received = lax.all_to_all(to_owners, every, split_axis=0, concat_axis=0, tiled=True)
    own_columns = received.reshape(seq_count, cores, 2, column_count).sum(axis=1)
    grad_mod = jnp.einsum(
        "sd,snc->ndc", all_cond.astype(F32), own_columns, precision=lax.Precision.HIGHEST
    )
    grad_bias = jnp.sum(own_columns, axis=0)

    grad_up = jnp.stack(
        [g.transpose(1, 0, 2).reshape(slab, count * unit_cols) for g in grad_up_list]
    )
    grad_down = jnp.stack(
        [g.transpose(0, 2, 1).reshape(count * unit_cols, slab) for g in grad_down_list]
    )
    grad_qkv = jnp.stack(
        [
            g[:, :, : 3 * head_cols]
            .reshape(count, slab, 3, head_cols)
            .transpose(1, 2, 0, 3)
            .reshape(slab, 3, count * head_cols)
            for g in grad_attn_list
        ]
    )
    grad_proj = jnp.stack(
        [
            g[:, :, 3 * head_cols :].transpose(0, 2, 1).reshape(count * head_cols, slab)
            for g in grad_attn_list
        ]
    )

    new_mod, mean_mod_next, second_mod_next = adam_step(mod_weight, grad_mod, mean_mod, second_mod)
    new_bias, mean_bias_next, second_bias_next = adam_step(
        mod_bias, grad_bias, mean_bias, second_bias
    )
    new_qkv, mean_qkv_next, second_qkv_next = adam_step(qkv_weight, grad_qkv, mean_qkv, second_qkv)
    new_proj, mean_proj_next, second_proj_next = adam_step(
        proj_weight, grad_proj, mean_proj, second_proj
    )
    new_up, mean_up_next, second_up_next = adam_step(up_weight, grad_up, mean_up, second_up)
    new_down, mean_down_next, second_down_next = adam_step(
        down_weight, grad_down, mean_down, second_down
    )
    return (
        image_out,
        text_out,
        image_grad,
        text_grad,
        grad_mod,
        grad_bias,
        grad_qkv,
        grad_proj,
        grad_up,
        grad_down,
        new_mod,
        new_bias,
        new_qkv,
        new_proj,
        new_up,
        new_down,
        mean_mod_next,
        second_mod_next,
        mean_bias_next,
        second_bias_next,
        mean_qkv_next,
        second_qkv_next,
        mean_proj_next,
        second_proj_next,
        mean_up_next,
        second_up_next,
        mean_down_next,
        second_down_next,
    )


def solution(mesh):
    dp, cores = mesh.devices.shape
    inner = math.gcd(dp, INNER)
    split = Mesh(mesh.devices.reshape(dp // inner, inner, cores), ("outer", "inner", "tensor"))
    group = ("outer", "inner")
    every = ("outer", "inner", "tensor")
    tokens = P(group, None, None)
    mod, bias = (P(None, None, every), P(None, every))
    qkv = P(None, group, None, "tensor")
    columns = P(None, group, "tensor")
    rows = P(None, "tensor", group)
    return jax.shard_map(
        local,
        mesh=split,
        in_specs=(tokens,) * 4
        + (P(),)
        + (mod, bias, qkv, rows, columns, rows)
        + (mod, mod, bias, bias, qkv, qkv, rows, rows, columns, columns, rows, rows),
        out_specs=(tokens,) * 4
        + (mod, bias, qkv, rows, columns, rows)
        + (mod, bias, qkv, rows, columns, rows)
        + (mod, mod, bias, bias, qkv, qkv, rows, rows, columns, columns, rows, rows),
        check_vma=False,
    )
```

```python
import functools
import math

import jax
import jax.numpy as jnp
from jax import lax
from jax.experimental import pallas as pl
from jax.experimental.pallas import tpu as pltpu
from jax.sharding import Mesh
from jax.sharding import PartitionSpec as P


HD = 64
ADAM_STEP = 10
INNER = 4

eps_norm = 1e-06
beta_one = 0.9
beta_two = 0.999
adam_eps = 1e-08
learn_rate = 0.02
decay_rate = 0.1
gelu_coef = 0.7978845608028654
cubic_coef = 0.044715
score_scale = 1.0 / math.sqrt(HD)
NEGATIVE = -1e30
LANES = 128
CHUNK = 16

F32 = jnp.float32
BF16 = jnp.bfloat16


def layer_norm(values):
    average = jnp.mean(values, axis=-1, keepdims=True)
    centred = values - average
    variance = jnp.mean(centred * centred, axis=-1, keepdims=True)
    inv_std = lax.rsqrt(variance + eps_norm)
    return (centred * inv_std, inv_std)


def norm_back(grad_normed, normed, inv_std):
    mean_grad = jnp.mean(grad_normed, axis=-1, keepdims=True)
    mean_cross = jnp.mean(grad_normed * normed, axis=-1, keepdims=True)
    return inv_std * (grad_normed - mean_grad - normed * mean_cross)


def gelu_pair(inputs):
    argument = gelu_coef * (inputs + cubic_coef * inputs * inputs * inputs)
    tangent = jnp.tanh(argument)
    activated = 0.5 * inputs * (1.0 + tangent)
    derivative = 0.5 * (1.0 + tangent) + 0.5 * inputs * (1.0 - tangent * tangent) * gelu_coef * (
        1.0 + 3.0 * cubic_coef * inputs * inputs
    )
    return (activated, derivative)


def adam_step(weight, gradient, mean_old, second_old):
    mean_new = beta_one * mean_old + (1.0 - beta_one) * gradient
    second_new = beta_two * second_old + (1.0 - beta_two) * gradient * gradient
    mean_hat = mean_new / (1.0 - beta_one**ADAM_STEP)
    second_hat = second_new / (1.0 - beta_two**ADAM_STEP)
    updated = weight - learn_rate * (
        mean_hat / (jnp.sqrt(second_hat) + adam_eps) + decay_rate * weight
    )
    return (updated, mean_new, second_new)


def dot_nn(a, b):
    return lax.dot_general(a, b, (((1,), (0,)), ((), ())), preferred_element_type=F32)


def dot_nt(a, b):
    return lax.dot_general(a, b, (((1,), (1,)), ((), ())), preferred_element_type=F32)


def dot_tn(a, b):
    return lax.dot_general(a, b, (((0,), (0,)), ((), ())), preferred_element_type=F32)


def key_bias(valid_ref, rows, padded):
    image, text = rows
    column = lax.broadcasted_iota(jnp.int32, (1, padded), 1)
    first = 2 * image
    second = first + text
    real = (column < first + valid_ref[0]) | ((column >= second) & (column < second + valid_ref[1]))
    return jnp.where(real, 0.0, NEGATIVE)


def pieces_of(rows):
    image, text = rows
    return ((0, image), (image, image), (2 * image, text), (2 * image + text, text))


def attend_kernel(rows, heads, padded, valid_ref, *refs):
    qkv, contexts, lse_ref, joint = (refs[:4], refs[4:8], refs[8], refs[9])
    width = heads * HD
    pieces = pieces_of(rows)
    total = 2 * sum(rows)
    for ref, (offset, size) in zip(qkv, pieces):
        joint[offset : offset + size, :] = ref[:, : 3 * width]
    if padded > total:
        joint[total:, :] = jnp.zeros((padded - total, 3 * width), BF16)
    bias = key_bias(valid_ref, rows, padded)
    for out in contexts:
        out[:, : 3 * width] = jnp.zeros((out.shape[0], 3 * width), BF16)
    for head in range(heads):
        at = head * HD
        keys = joint[:, width + at : width + at + HD]
        values = joint[:, 2 * width + at : 2 * width + at + HD]
        for ref, out, (offset, size) in zip(qkv, contexts, pieces):
            scores = dot_nt(ref[:, at : at + HD], keys) * score_scale + bias
            highest = jnp.max(scores, axis=-1, keepdims=True)
            weights = jnp.exp(scores - highest)
            totals = jnp.sum(weights, axis=-1, keepdims=True)
            probs = (weights * (1.0 / totals)).astype(BF16)
            out[:, 3 * width + at : 3 * width + at + HD] = dot_nn(probs, values).astype(BF16)
            lse_ref[offset : offset + size, head : head + 1] = highest + jnp.log(totals)


def attend_back_kernel(rows, heads, padded, valid_ref, *refs):
    qkv, contexts, grads, lse_ref = (refs[:4], refs[4:8], refs[8:12], refs[12])
    outs, joint, key_sum, value_sum = (refs[13:17], refs[17], refs[18], refs[19])
    width = heads * HD
    pieces = pieces_of(rows)
    total = 2 * sum(rows)
    for ref, (offset, size) in zip(qkv, pieces):
        joint[offset : offset + size, :] = ref[:, : 3 * width]
    if padded > total:
        joint[total:, :] = jnp.zeros((padded - total, 3 * width), BF16)
    for out in outs:
        out[:, 3 * width :] = jnp.zeros((out.shape[0], width), BF16)
    bias = key_bias(valid_ref, rows, padded)
    for head in range(heads):
        at = head * HD
        keys = joint[:, width + at : width + at + HD]
        values = joint[:, 2 * width + at : 2 * width + at + HD]
        for number, (offset, size) in enumerate(pieces):
            queries = qkv[number][:, at : at + HD]
            grad_context = grads[number][:, 3 * width + at : 3 * width + at + HD]
            context = contexts[number][:, 3 * width + at : 3 * width + at + HD]
            scores = dot_nt(queries, keys) * score_scale + bias
            probs = jnp.exp(scores - lse_ref[offset : offset + size, head : head + 1])
            grad_probs = dot_nt(grad_context, values)
            row_dots = jnp.sum(
                grad_context.astype(F32) * context.astype(F32), axis=-1, keepdims=True
            )
            grad_scores = (probs * (grad_probs - row_dots) * score_scale).astype(BF16)
            outs[number][:, at : at + HD] = dot_nn(grad_scores, keys).astype(BF16)
            value_part = dot_tn(probs.astype(BF16), grad_context)
            key_part = dot_tn(grad_scores, queries)
            if number == 0:
                value_sum[...] = value_part
                key_sum[...] = key_part
            else:
                value_sum[...] += value_part
                key_sum[...] += key_part
        for number, (offset, size) in enumerate(pieces):
            outs[number][:, width + at : width + at + HD] = key_sum[
                offset : offset + size, :
            ].astype(BF16)
            outs[number][:, 2 * width + at : 2 * width + at + HD] = value_sum[
                offset : offset + size, :
            ].astype(BF16)


def piece_specs(rows, columns):
    image, text = rows
    return [pl.BlockSpec((size, columns), lambda s, v: (s, 0)) for size in (image, image, text, text)]


def attend(rows, heads, seqs, valid, qkv):
    total = 2 * sum(rows)
    padded = -(-total // LANES) * LANES
    width = heads * HD
    sizes = (rows[0], rows[0], rows[1], rows[1])
    return pl.pallas_call(
        functools.partial(attend_kernel, rows, heads, padded),
        grid_spec=pltpu.PrefetchScalarGridSpec(
            num_scalar_prefetch=1,
            grid=(seqs,),
            in_specs=piece_specs(rows, qkv[0].shape[1]),
            out_specs=piece_specs(rows, 4 * width)
            + [pl.BlockSpec((None, total, LANES), lambda s, v: (s, 0, 0))],
            scratch_shapes=[pltpu.VMEM((padded, 3 * width), BF16)],
        ),
        out_shape=[jax.ShapeDtypeStruct((seqs * size, 4 * width), BF16) for size in sizes]
        + [jax.ShapeDtypeStruct((seqs, total, LANES), F32)],
        cost_estimate=pl.CostEstimate(
            flops=4 * seqs * heads * total * total * HD,
            bytes_accessed=8 * seqs * total * width,
            transcendentals=seqs * heads * total * total,
        ),
        name="attend",
    )(valid, *qkv)


def attend_back(rows, heads, seqs, valid, qkv, contexts, grads, lse):
    total = 2 * sum(rows)
    padded = -(-total // LANES) * LANES
    width = heads * HD
    sizes = (rows[0], rows[0], rows[1], rows[1])
    return pl.pallas_call(
        functools.partial(attend_back_kernel, rows, heads, padded),
        grid_spec=pltpu.PrefetchScalarGridSpec(
            num_scalar_prefetch=1,
            grid=(seqs,),
            in_specs=piece_specs(rows, qkv[0].shape[1])
            + piece_specs(rows, 4 * width)
            + piece_specs(rows, 4 * width)
            + [pl.BlockSpec((None, total, LANES), lambda s, v: (s, 0, 0))],
            out_specs=piece_specs(rows, 4 * width),
            scratch_shapes=[
                pltpu.VMEM((padded, 3 * width), BF16),
                pltpu.VMEM((padded, HD), F32),
                pltpu.VMEM((padded, HD), F32),
            ],
        ),
        out_shape=[jax.ShapeDtypeStruct((seqs * size, 4 * width), BF16) for size in sizes],
        cost_estimate=pl.CostEstimate(
            flops=10 * seqs * heads * total * total * HD,
            bytes_accessed=20 * seqs * total * width,
            transcendentals=seqs * heads * total * total,
        ),
        name="attend_back",
    )(valid, *qkv, *contexts, *grads, lse)


def swap_core(values):
    return lax.ppermute(values, "tensor", [(0, 1), (1, 0)])


def hop(values, distance, count):
    return lax.ppermute(values, "inner", [(i, i ^ distance) for i in range(count)])


def start_rows(rows, count):
    return [rows] + [hop(rows, j, count) for j in range(1, count)]


def finish_rows(blocks):
    own = jnp.concatenate(blocks, axis=0)
    return (own, swap_core(own))


def gather_rows(rows, count):
    return finish_rows(start_rows(rows, count))


def finish_both(blocks, image):
    return [
        finish_rows([block[part] for block in blocks])
        for part in (slice(image), slice(image, None))
    ]


def send_rows(own, other, count):
    arrived = swap_core(other.astype(BF16))
    blocks = (own + arrived.astype(F32)).reshape(count, own.shape[0] // count, own.shape[1])
    low = blocks.astype(BF16)
    return (blocks[0], [hop(low[j], j, count) for j in range(1, count)])


def add_rows(sent):
    total, parts = sent
    for part in parts:
        total = total + part.astype(F32)
    return total


def send_both(partials, count):
    arrived = swap_core(jnp.concatenate([p[1].astype(BF16) for p in partials], axis=0))
    middle = partials[0][0].shape[0]
    sums = [
        (p[0] + part.astype(F32)).reshape(count, p[0].shape[0] // count, p[0].shape[1])
        for p, part in zip(partials, (arrived[:middle], arrived[middle:]))
    ]
    lows = [
        jnp.concatenate([part[j].astype(BF16) for part in sums], axis=0)
        for j in range(1, count)
    ]
    return ([part[0] for part in sums], [hop(lows[j - 1], j, count) for j in range(1, count)])


def by_place(me_ref, count, body):
    for number in range(count):
        pl.when(me_ref[0] == number)(functools.partial(body, number))


def pack_attn_kernel(count, me_ref, qkv_ref, proj_ref, *outs):
    columns = proj_ref.shape[2] // count

    def place(number):
        for j, out in enumerate(outs):
            at = (j ^ number) * columns
            for n in range(2):
                base = 4 * n * columns
                for k in range(3):
                    out[:, base + k * columns : base + (k + 1) * columns] = qkv_ref[
                        n, k, :, at : at + columns
                    ].astype(BF16)
                out[:, base + 3 * columns : base + 4 * columns] = proj_ref[
                    n, :, at : at + columns
                ].astype(BF16)

    by_place(me_ref, count, place)


def pack_attn(me, qkv, proj, count):
    slab, full = proj.shape[1:]
    shape = jax.ShapeDtypeStruct((slab, 8 * full // count), BF16)
    return pl.pallas_call(
        functools.partial(pack_attn_kernel, count),
        grid_spec=pltpu.PrefetchScalarGridSpec(
            num_scalar_prefetch=1,
            grid=(1,),
            in_specs=[
                pl.BlockSpec(qkv.shape, lambda i, m: (0, 0, 0, 0)),
                pl.BlockSpec(proj.shape, lambda i, m: (0, 0, 0)),
            ],
            out_specs=[pl.BlockSpec(shape.shape, lambda i, m: (0, 0))] * count,
        ),
        out_shape=[shape] * count,
    )(me, qkv, proj)


def pack_ff_kernel(count, me_ref, up_ref, down_ref, *outs):
    columns = up_ref.shape[1] // count

    def place(number):
        for j, out in enumerate(outs):
            at = (j ^ number) * columns
            out[:, :columns] = up_ref[:, at : at + columns].astype(BF16)
            out[:, columns:] = down_ref[:, at : at + columns].astype(BF16)

    by_place(me_ref, count, place)


def pack_ff(me, up, down, n, count):
    slab, full = up.shape[1:]
    shape = jax.ShapeDtypeStruct((slab, 2 * full // count), BF16)
    spec = pl.BlockSpec((None, slab, full), lambda i, m: (n, 0, 0))
    return pl.pallas_call(
        functools.partial(pack_ff_kernel, count),
        grid_spec=pltpu.PrefetchScalarGridSpec(
            num_scalar_prefetch=1,
            grid=(1,),
            in_specs=[spec, spec],
            out_specs=[pl.BlockSpec(shape.shape, lambda i, m: (0, 0))] * count,
        ),
        out_shape=[shape] * count,
    )(me, up, down)


def unpack_kernel(count, me_ref, *refs):
    blocks, out = (refs[:count], refs[count])
    slab = blocks[0].shape[0]

    def place(number):
        for j, block in enumerate(blocks):
            at = (j ^ number) * slab
            out[at : at + slab, :] = block[...]

    by_place(me_ref, count, place)


def unpack(me, blocks):
    count = len(blocks)
    slab, columns = blocks[0].shape
    return pl.pallas_call(
        functools.partial(unpack_kernel, count),
        grid_spec=pltpu.PrefetchScalarGridSpec(
            num_scalar_prefetch=1,
            grid=(1,),
            in_specs=[pl.BlockSpec((slab, columns), lambda i, m: (0, 0))] * count,
            out_specs=pl.BlockSpec((count * slab, columns), lambda i, m: (0, 0)),
        ),
        out_shape=jax.ShapeDtypeStruct((count * slab, columns), BF16),
    )(me, *blocks)


def adam_refs(gradient, weight, mean, second, outs):
    updated, mean_new, second_new = adam_step(weight, gradient, mean, second)
    for out, value in zip(outs, (gradient, updated, mean_new, second_new)):
        out[...] = value


def adam_ff_kernel(count, me_ref, *refs):
    blocks, (weight, mean, second) = (refs[:count], refs[count : count + 3])
    outs, gradient = (refs[-5:-1], refs[-1])
    wanted = pl.program_id(0) ^ me_ref[0]
    for j, block in enumerate(blocks):

        @pl.when(wanted == j)
        def take(block=block):
            gradient[...] = block[...].astype(F32)

    adam_refs(gradient[...], weight[...], mean[...], second[...], outs)


def adam_ff(me, blocks, half, weight, mean, second, n, before):
    count = len(blocks)
    slab, columns = (blocks[0].shape[0], blocks[0].shape[1] // 2)
    spec = pl.BlockSpec((None, slab, columns), lambda c, m: (n, 0, c))
    return pl.pallas_call(
        functools.partial(adam_ff_kernel, count),
        grid_spec=pltpu.PrefetchScalarGridSpec(
            num_scalar_prefetch=1,
            grid=(count,),
            in_specs=[pl.BlockSpec((slab, columns), lambda c, m: (0, half))] * count
            + [spec] * 3
            + [pl.BlockSpec(memory_space=pl.ANY)] * len(before),
            out_specs=[spec] * 4,
            scratch_shapes=[pltpu.VMEM((slab, columns), F32)],
        ),
        out_shape=[jax.ShapeDtypeStruct(weight.shape, F32)] * 4,
        input_output_aliases={1 + count + 3 + i: i for i in range(len(before))},
    )(me, *blocks, weight, mean, second, *before)


def adam_attn_kernel(count, me_ref, *refs):
    blocks, weights = (refs[:count], refs[count : count + 6])
    qkv_outs, proj_outs = (refs[-10:-6], refs[-6:-2])
    qkv_grad, proj_grad = refs[-2:]
    columns = proj_grad.shape[1] // count

    def place(number):
        for j, block in enumerate(blocks):
            at = (j ^ number) * columns
            for k in range(3):
                qkv_grad[k, :, at : at + columns] = block[
                    :, k * columns : (k + 1) * columns
                ].astype(F32)
            proj_grad[:, at : at + columns] = block[:, 3 * columns :].astype(F32)

    by_place(me_ref, count, place)
    adam_refs(qkv_grad[...], weights[0][...], weights[1][...], weights[2][...], qkv_outs)
    adam_refs(proj_grad[...], weights[3][...], weights[4][...], weights[5][...], proj_outs)


def adam_attn(me, blocks, qkv, proj, n, before):
    count = len(blocks)
    slab, full = proj[0].shape[1:]
    qkv_spec = pl.BlockSpec((None, 3, slab, full), lambda i, m: (n, 0, 0, 0))
    proj_spec = pl.BlockSpec((None, slab, full), lambda i, m: (n, 0, 0))
    return pl.pallas_call(
        functools.partial(adam_attn_kernel, count),
        grid_spec=pltpu.PrefetchScalarGridSpec(
            num_scalar_prefetch=1,
            grid=(1,),
            in_specs=[pl.BlockSpec(blocks[0].shape, lambda i, m: (0, 0))] * count
            + [qkv_spec] * 3
            + [proj_spec] * 3
            + [pl.BlockSpec(memory_space=pl.ANY)] * len(before),
            out_specs=[qkv_spec] * 4 + [proj_spec] * 4,
            scratch_shapes=[pltpu.VMEM((3, slab, full), F32), pltpu.VMEM((slab, full), F32)],
        ),
        out_shape=[jax.ShapeDtypeStruct(qkv[0].shape, F32)] * 4
        + [jax.ShapeDtypeStruct(proj[0].shape, F32)] * 4,
        input_output_aliases={1 + count + 6 + i: i for i in range(len(before))},
    )(me, *blocks, *qkv, *proj, *before)


def exchange(blocks, count):
    return [blocks[0]] + [hop(blocks[j], j, count) for j in range(1, count)]


def after(values, *done):
    return jax.tree.map(lambda value: lax.optimization_barrier((value, done))[0], values)


def whole(array):
    return pl.BlockSpec(array.shape, lambda i, m: (0,) * len(array.shape))


def row_kernel(body, place, inputs, outputs, scratch=()):
    return pl.pallas_call(
        body,
        grid_spec=pltpu.PrefetchScalarGridSpec(
            num_scalar_prefetch=1,
            grid=(1,),
            in_specs=[whole(a) for a in inputs],
            out_specs=[whole(a) for a in outputs],
            scratch_shapes=list(scratch),
        ),
        out_shape=list(outputs),
    )(place, *inputs)


def fold(values):
    return jnp.sum(values.reshape(values.shape[0] // 8, 8, values.shape[1]), axis=0)


def arrived_rows(own, parts, where, offset):
    total = own[where, :]
    for part in parts:
        total = total + part[pl.ds(pl.multiple_of(offset, CHUNK), CHUNK), :].astype(F32)
    return total


def middle_back_kernel(n, me_ref, own, *refs):
    parts, (middle, attn, cotangent, mods) = (refs[:-7], refs[-7:-3])
    grad_out, low_out, sums_out = refs[-3:]
    zero = jnp.zeros((8, own.shape[1]), F32)
    scale, gate = (mods[n, 4:5, :], mods[n, 2:3, :])

    def step(i, sums):
        where = pl.ds(pl.multiple_of(i * CHUNK, CHUNK), CHUNK)
        grad = arrived_rows(own, parts, where, i * CHUNK)
        normed, inv_std = layer_norm(middle[where, :])
        total = cotangent[where, :].astype(F32) + norm_back(grad * (1.0 + scale), normed, inv_std)
        grad_out[where, :] = total
        low_out[where, :] = (total * gate).astype(BF16)
        terms = (total * attn[where, :], grad, grad * normed)
        return tuple(a + fold(b) for a, b in zip(sums, terms))

    sums = lax.fori_loop(0, own.shape[0] // CHUNK, step, (zero,) * 3)
    for k, value in enumerate(sums):
        sums_out[k : k + 1, :] = jnp.sum(value, axis=0, keepdims=True)


def middle_back(place, n, sent, middle, attn, cotangent, mods):
    own, parts = sent
    return row_kernel(
        functools.partial(middle_back_kernel, n),
        place,
        (own, *parts, middle, attn, cotangent, mods),
        (
            jax.ShapeDtypeStruct(own.shape, F32),
            jax.ShapeDtypeStruct(own.shape, BF16),
            jax.ShapeDtypeStruct((8, own.shape[1]), F32),
        ),
    )


def end_kernel(arrivals, me_ref, *refs):
    mods, back = (refs[0], refs[1 : 1 + arrivals])
    streams = refs[1 + arrivals : -4]
    each = len(streams) // 2
    grads_out, rows_out, owners_out, table = refs[-4:]
    offset = 0
    for n in range(2):
        own, tokens, grad_middle, cotangent, middle, sums, down = streams[n * each :][:7]
        parts = streams[n * each + 7 : (n + 1) * each]
        zero = jnp.zeros((8, own.shape[1]), F32)
        scale, gate = (mods[n, 1:2, :], mods[n, 5:6, :])

        def step(i, totals):
            where = pl.ds(pl.multiple_of(i * CHUNK, CHUNK), CHUNK)
            place = pl.ds(pl.multiple_of(offset + i * CHUNK, CHUNK), CHUNK)
            grad = arrived_rows(own, back, where, offset + i * CHUNK)
            normed, inv_std = layer_norm(tokens[where, :].astype(F32))
            grads_out[place, :] = grad_middle[where, :] + norm_back(
                grad * (1.0 + scale), normed, inv_std
            )
            total = arrived_rows(down, parts, where, i * CHUNK)
            rows_out[place, :] = middle[where, :] + gate * total
            terms = (grad, grad * normed, cotangent[where, :].astype(F32) * total)
            return tuple(a + fold(b) for a, b in zip(totals, terms))

        totals = lax.fori_loop(0, own.shape[0] // CHUNK, step, (zero,) * 3)
        for k, value in zip((0, 1, 5), totals):
            table[6 * n + k : 6 * n + k + 1, :] = jnp.sum(value, axis=0, keepdims=True)
        table[6 * n + 2 : 6 * n + 5, :] = sums[0:3, :]
        offset += own.shape[0]
    width = table.shape[1]
    devices, _, columns = owners_out.shape
    for n in range(2):
        for d in range(devices):
            done = 0
            while done < columns:
                k, at = divmod(d * columns + done, width)
                size = min(columns - done, width - at)
                owners_out[d, n : n + 1, done : done + size] = table[
                    6 * n + k : 6 * n + k + 1, at : at + size
                ]
                done += size


def end_rows(place, mods, sent_one, streams, down_sent, devices):
    owns, back = sent_one
    inputs = [mods, *back]
    for n in range(2):
        inputs += [owns[n], *streams[n], down_sent[n][0], *down_sent[n][1]]
    rows, width = back[0].shape
    columns = 6 * width // devices
    return row_kernel(
        functools.partial(end_kernel, len(back)),
        place,
        inputs,
        (
            jax.ShapeDtypeStruct((rows, width), F32),
            jax.ShapeDtypeStruct((rows, width), F32),
            jax.ShapeDtypeStruct((devices, 2, columns), F32),
        ),
        (pltpu.VMEM((16, width), F32),),
    )


def whole_rows_kernel(core_ref, own, other, *outs):
    for core in range(2):

        @pl.when(core_ref[0] == core)
        def place(core=core):
            start = 0
            for out in outs:
                length = out.shape[1]
                size = (own.shape[0] - start) if start else length // 2
                for number, source in ((core, own), (1 - core, other)):
                    count = min(size, length - number * size)
                    out[0, number * size : number * size + count, :] = source[
                        start : start + count, :
                    ]
                start += size


def whole_rows(core, own, lengths):
    return row_kernel(
        whole_rows_kernel,
        core,
        (own, swap_core(own)),
        [jax.ShapeDtypeStruct((1, length, own.shape[1]), F32) for length in lengths],
    )


def attn_gradient_kernel(columns, me_ref, *refs):
    shifted, grads, proj_ins, contexts, out = (refs[:2], refs[2:4], refs[4:6], refs[6:8], refs[8])
    full = out.shape[1]
    split = columns // 256 * 256
    for low, high in ((0, split), (split, full)):
        total = None
        terms = list(zip(shifted, grads))
        if high > columns:
            terms += list(zip(proj_ins, contexts))
        for left, right in terms:
            part = dot_tn(left[...], right[:, low:high])
            total = part if total is None else total + part
        out[:, low:high] = total.astype(BF16)


def attn_gradient(place, columns, shifted, grads, proj_ins, contexts):
    width = shifted[0].shape[1]
    full = grads[0].shape[1]
    tile = math.gcd(512, width)
    left = [pl.BlockSpec((a.shape[0], tile), lambda i, m: (0, i)) for a in shifted]
    right = [pl.BlockSpec(a.shape, lambda i, m: (0, 0)) for a in grads]
    rows = shifted[0].shape[0]
    return pl.pallas_call(
        functools.partial(attn_gradient_kernel, columns),
        grid_spec=pltpu.PrefetchScalarGridSpec(
            num_scalar_prefetch=1,
            grid=(width // tile,),
            in_specs=(left + right) * 2,
            out_specs=pl.BlockSpec((tile, full), lambda i, m: (i, 0)),
        ),
        out_shape=jax.ShapeDtypeStruct((width, full), BF16),
        cost_estimate=pl.CostEstimate(
            flops=4 * rows * width * full, bytes_accessed=8 * rows * width, transcendentals=0
        ),
    )(place, *shifted, *grads, *proj_ins, *contexts)


def local(
    image_tokens,
    text_tokens,
    image_cotangent,
    text_cotangent,
    timesteps,
    mod_weight,
    mod_bias,
    qkv_weight,
    proj_weight,
    up_weight,
    down_weight,
    mean_mod,
    second_mod,
    mean_bias,
    second_bias,
    mean_qkv,
    second_qkv,
    mean_proj,
    second_proj,
    mean_up,
    second_up,
    mean_down,
    second_down,
):
    count = lax.axis_size("inner")
    cores = lax.axis_size("tensor")
    me = lax.axis_index("inner")
    core = lax.axis_index("tensor")
    every = ("outer", "inner", "tensor")
    streams = (0, 1)
    seq_count = timesteps.shape[0]
    devices = seq_count * cores
    column_count = mod_weight.shape[2]
    width = image_tokens.shape[2]
    slab = qkv_weight.shape[1]
    head_cols = qkv_weight.shape[3] // count
    heads = head_cols // HD
    unit_cols = up_weight.shape[2] // count
    lengths = (image_tokens.shape[1], text_tokens.shape[1])
    rows = tuple(-(-length // (16 * cores)) * 16 for length in lengths)

    place = me.astype(jnp.int32)[None]
    qkv_all = [a.transpose(0, 2, 1, 3) for a in (qkv_weight, mean_qkv, second_qkv)]
    proj_all = [a.transpose(0, 2, 1) for a in (proj_weight, mean_proj, second_proj)]
    up_all = (up_weight, mean_up, second_up)
    down_all = [a.transpose(0, 2, 1) for a in (down_weight, mean_down, second_down)]

    def full_weight(shard):
        return lax.all_gather(shard, "outer", axis=0, tiled=True)

    blocks = pack_attn(place, qkv_all[0], proj_all[0], count)
    shard = unpack(place, exchange(blocks, count))
    attn_both = full_weight(shard)

    half_width = width // 2
    frequency = jnp.exp(-math.log(10000.0) * jnp.arange(half_width, dtype=F32) / half_width)
    angles = timesteps.astype(F32)[:, None] * frequency[None, :]
    all_cond = jax.nn.silu(jnp.concatenate([jnp.cos(angles), jnp.sin(angles)], axis=1)).astype(BF16)
    bias_low = lax.optimization_barrier(mod_bias.astype(BF16)).astype(F32)
    local_mod = (
        jnp.einsum("sd,ndc->snc", all_cond, mod_weight.astype(BF16), preferred_element_type=F32)
        + bias_low[None, :, :]
    )
    to_cores = jnp.broadcast_to(
        local_mod[:, None], (seq_count, cores, 2, column_count)
    ).reshape(devices, 2, column_count)
    spread = lax.all_to_all(to_cores, every, split_axis=0, concat_axis=0, tiled=True)
    mods = after(spread, shard).transpose(1, 0, 2).reshape(2, 6, width)

    def own_rows(tokens, size):
        short = cores * size - tokens.shape[1]
        padded = jnp.pad(tokens[0], ((0, short), (0, 0)))
        return lax.dynamic_slice(padded, (core * size, 0), (size, width))

    tokens = [own_rows(t, r) for t, r in zip((image_tokens, text_tokens), rows)]
    inputs = [t.astype(F32) for t in tokens]
    cotangents = [own_rows(t, r) for t, r in zip((image_cotangent, text_cotangent), rows)]
    valid = jnp.stack(
        [
            jnp.clip(lengths[1] - core * rows[1], 0, rows[1]),
            jnp.clip(lengths[1] - (1 - core) * rows[1], 0, rows[1]),
        ]
    ).astype(jnp.int32)

    shifted_one = []
    for n in streams:
        normed, _ = layer_norm(inputs[n])
        shifted_one.append((normed * (1.0 + mods[n, 1]) + mods[n, 0]).astype(BF16))
    shifted_one = finish_both(start_rows(jnp.concatenate(shifted_one, axis=0), count), rows[0])

    def ff_blocks(n, where):
        return exchange(pack_ff(where, up_all[0], down_all[0], n, count), count)

    shard = unpack(place, ff_blocks(0, after(place, shifted_one)))
    ff_full = [full_weight(shard)]
    blocks = ff_blocks(1, after(place, shard))
    gated = [
        (after(cotangents[n], shard).astype(F32) * mods[n, 5]).astype(BF16) for n in streams
    ]
    gated = start_rows(jnp.concatenate(gated, axis=0), count)

    wide = 4 * head_cols
    attn_full = [attn_both[:, :wide], attn_both[:, wide:]]
    qkv_pieces = [
        dot_nn(half, attn_full[n]).astype(BF16) for n in streams for half in shifted_one[n]
    ]
    *context_pieces, lse = attend(rows, heads, count, valid, qkv_pieces)
    contexts = (context_pieces[:2], context_pieces[2:])
    ff_full.append(full_weight(unpack(place, after(blocks, context_pieces))))
    attn_sums, middles, shifted_two, middle_rows = ([], [], [], [])
    for n in streams:
        partial = [dot_nt(half, attn_full[n]) for half in contexts[n]]
        attn_sum = add_rows(send_rows(partial[0], partial[1], count))
        middle = inputs[n] + mods[n, 2] * attn_sum
        normed, _ = layer_norm(middle)
        shifted = (normed * (1.0 + mods[n, 4]) + mods[n, 3]).astype(BF16)
        attn_sums.append(attn_sum)
        middles.append(middle)
        middle_rows.append(shifted)
        shifted_two.append(gather_rows(shifted, count))

    def outer_sum(gradient):
        return lax.psum_scatter(gradient, "outer", scatter_dimension=0, tiled=True)

    def owned(summed):
        return exchange(
            [
                lax.dynamic_slice(summed, ((me ^ j) * slab, 0), (slab, summed.shape[1]))
                for j in range(count)
            ],
            count,
        )

    down_ins = finish_both(after(gated, middle_rows[0]), rows[0])
    ff_full[0] = after(ff_full[0], middle_rows[0])
    grad_contexts, grad_middles, partial_rows, proj_ins = ([], [], [], [])
    ff_sums = []
    for n in streams:
        full = ff_full[n] if n == 0 else after(ff_full[n], proj_in, down_partials)
        up_full, down_full = (full[:, :unit_cols], full[:, unit_cols:])
        pairs = [gelu_pair(dot_nn(half, up_full)) for half in shifted_two[n]]
        hidden = [pair[0].astype(BF16) for pair in pairs]

        def down_gradient(where):
            total = dot_tn(where[0], hidden[0]) + dot_tn(where[1], hidden[1])
            return total.astype(BF16)

        grad_ins = down_ins[n]
        if n == 1:
            grad_down = down_gradient(grad_ins)
            grad_ins = after(grad_ins, grad_down)
        grad_pres = [
            (dot_nn(down_in, down_full) * pair[1]).astype(BF16)
            for down_in, pair in zip(grad_ins, pairs)
        ]
        partial = [dot_nt(grad_pre, up_full) for grad_pre in grad_pres]
        sent = send_rows(partial[0], partial[1], count)
        if n == 0:
            grad_down = down_gradient(after(grad_ins, partial))
            partial = (partial, grad_down)
        grad_pres = after(grad_pres, partial)
        total = dot_tn(shifted_two[n][0], grad_pres[0]) + dot_tn(shifted_two[n][1], grad_pres[1])
        grad_up = total.astype(BF16)
        ff_sums.append(outer_sum(jnp.concatenate([grad_down, grad_up], axis=1)))
        grad_middle, proj_in, sums = middle_back(
            place, n, after(sent, grad_up), middles[n], attn_sums[n], cotangents[n], mods
        )
        halves = gather_rows(proj_in, count)
        grad_contexts += [dot_nn(half, attn_full[n]).astype(BF16) for half in halves]
        proj_ins.append(halves)
        grad_middles.append(grad_middle)
        partial_rows.append(sums)
        if n == 0:
            down_partials = [dot_nt(half, down_full) for half in after(hidden, proj_in)]
    down_sent = send_rows(down_partials[0], down_partials[1], count)
    ff_sums[0] = after(ff_sums[0], grad_contexts)

    grad_pieces = attend_back(
        rows, heads, count, valid, qkv_pieces, context_pieces, grad_contexts, lse
    )
    grad_qkv_rows = (grad_pieces[:2], grad_pieces[2:])
    grad_attn = []
    for n in streams:
        grad_attn.append(
            attn_gradient(
                place, 3 * head_cols, shifted_one[n], grad_qkv_rows[n], proj_ins[n], contexts[n]
            )
        )
    attn_grad_sums = [outer_sum(grad_attn[n]) for n in streams]
    grad_qkv_rows = after(grad_qkv_rows, grad_attn)
    partials = [[dot_nt(half, attn_full[n]) for half in grad_qkv_rows[n]] for n in streams]
    sent_one = send_both(partials, count)
    hidden, down_sent = after((hidden, down_sent), partials)
    down_partials = [dot_nt(half, down_full) for half in hidden]
    down_sent = [down_sent, send_rows(down_partials[0], down_partials[1], count)]

    def adam_both(n, before):
        blocks = owned(ff_sums[n])
        return [
            adam_ff(place, blocks, half, *arrays, n, outs)
            for half, arrays, outs in zip((0, 1), (down_all, up_all), before)
        ]

    ff_outs = adam_both(0, ((), ()))
    grad_rows, out_rows, to_owners = end_rows(
        place,
        mods,
        after(sent_one, down_partials, ff_outs[0][0], ff_outs[1][0]),
        [
            (tokens[n], grad_middles[n], cotangents[n], middles[n], partial_rows[n])
            for n in streams
        ],
        down_sent,
        devices,
    )

    received = lax.all_to_all(to_owners, every, split_axis=0, concat_axis=0, tiled=True)
    own_columns = received.reshape(seq_count, cores, 2, column_count).sum(axis=1)
    grad_mod = jnp.einsum(
        "sd,snc->ndc", all_cond.astype(F32), own_columns, precision=lax.Precision.HIGHEST
    )
    grad_bias = jnp.sum(own_columns, axis=0)
    new_mod, mean_mod_next, second_mod_next = adam_step(mod_weight, grad_mod, mean_mod, second_mod)
    new_bias, mean_bias_next, second_bias_next = adam_step(
        mod_bias, grad_bias, mean_bias, second_bias
    )

    core_place = core.astype(jnp.int32)[None]
    image_out, text_out = whole_rows(core_place, out_rows, lengths)
    image_grad, text_grad = whole_rows(core_place, grad_rows, lengths)

    ff_sums[1] = after(ff_sums[1], to_owners)
    ff_outs = adam_both(1, ff_outs)
    down_outs, up_outs = ff_outs
    attn_outs = adam_attn(
        place, owned(after(attn_grad_sums[0], to_owners)), qkv_all, proj_all, 0, ()
    )
    last_sum = after(
        attn_grad_sums[1], attn_outs[0], up_outs[0], down_outs[0], new_mod, text_out, text_grad
    )
    attn_outs = adam_attn(place, owned(last_sum), qkv_all, proj_all, 1, attn_outs)
    grad_up, new_up, mean_up_next, second_up_next = up_outs
    grad_down, new_down, mean_down_next, second_down_next = (
        a.transpose(0, 2, 1) for a in down_outs
    )
    grad_qkv, new_qkv, mean_qkv_next, second_qkv_next = (
        a.transpose(0, 2, 1, 3) for a in attn_outs[:4]
    )
    grad_proj, new_proj, mean_proj_next, second_proj_next = (
        a.transpose(0, 2, 1) for a in attn_outs[4:]
    )
    return (
        image_out,
        text_out,
        image_grad,
        text_grad,
        grad_mod,
        grad_bias,
        grad_qkv,
        grad_proj,
        grad_up,
        grad_down,
        new_mod,
        new_bias,
        new_qkv,
        new_proj,
        new_up,
        new_down,
        mean_mod_next,
        second_mod_next,
        mean_bias_next,
        second_bias_next,
        mean_qkv_next,
        second_qkv_next,
        mean_proj_next,
        second_proj_next,
        mean_up_next,
        second_up_next,
        mean_down_next,
        second_down_next,
    )


def solution(mesh):
    dp, cores = mesh.devices.shape
    inner = math.gcd(dp, INNER)
    split = Mesh(mesh.devices.reshape(dp // inner, inner, cores), ("outer", "inner", "tensor"))
    group = ("outer", "inner")
    every = ("outer", "inner", "tensor")
    tokens = P(group, None, None)
    mod, bias = (P(None, None, every), P(None, every))
    qkv = P(None, group, None, "tensor")
    columns = P(None, group, "tensor")
    rows = P(None, "tensor", group)
    return jax.shard_map(
        local,
        mesh=split,
        in_specs=(tokens,) * 4
        + (P(),)
        + (mod, bias, qkv, rows, columns, rows)
        + (mod, mod, bias, bias, qkv, qkv, rows, rows, columns, columns, rows, rows),
        out_specs=(tokens,) * 4
        + (mod, bias, qkv, rows, columns, rows)
        + (mod, bias, qkv, rows, columns, rows)
        + (mod, mod, bias, bias, qkv, qkv, rows, rows, columns, columns, rows, rows),
        check_vma=False,
    )
```

```python
import functools
import math

import jax
import jax.numpy as jnp
from jax import lax
from jax.experimental import pallas as pl
from jax.experimental.pallas import tpu as pltpu
from jax.sharding import Mesh
from jax.sharding import PartitionSpec as P


HD = 64
ADAM_STEP = 10
INNER = 4

eps_norm = 1e-06
beta_one = 0.9
beta_two = 0.999
adam_eps = 1e-08
learn_rate = 0.02
decay_rate = 0.1
gelu_coef = 0.7978845608028654
cubic_coef = 0.044715
score_scale = 1.0 / math.sqrt(HD)
NEGATIVE = -1e30
LANES = 128
CHUNK = 16

F32 = jnp.float32
BF16 = jnp.bfloat16


def layer_norm(values):
    average = jnp.mean(values, axis=-1, keepdims=True)
    centred = values - average
    variance = jnp.mean(centred * centred, axis=-1, keepdims=True)
    inv_std = lax.rsqrt(variance + eps_norm)
    return (centred * inv_std, inv_std)


def norm_back(grad_normed, normed, inv_std):
    mean_grad = jnp.mean(grad_normed, axis=-1, keepdims=True)
    mean_cross = jnp.mean(grad_normed * normed, axis=-1, keepdims=True)
    return inv_std * (grad_normed - mean_grad - normed * mean_cross)


def gelu_pair(inputs):
    argument = gelu_coef * (inputs + cubic_coef * inputs * inputs * inputs)
    tangent = jnp.tanh(argument)
    activated = 0.5 * inputs * (1.0 + tangent)
    derivative = 0.5 * (1.0 + tangent) + 0.5 * inputs * (1.0 - tangent * tangent) * gelu_coef * (
        1.0 + 3.0 * cubic_coef * inputs * inputs
    )
    return (activated, derivative)


def adam_step(weight, gradient, mean_old, second_old):
    mean_new = beta_one * mean_old + (1.0 - beta_one) * gradient
    second_new = beta_two * second_old + (1.0 - beta_two) * gradient * gradient
    mean_hat = mean_new / (1.0 - beta_one**ADAM_STEP)
    second_hat = second_new / (1.0 - beta_two**ADAM_STEP)
    updated = weight - learn_rate * (
        mean_hat / (jnp.sqrt(second_hat) + adam_eps) + decay_rate * weight
    )
    return (updated, mean_new, second_new)


def dot_nn(a, b):
    return lax.dot_general(a, b, (((1,), (0,)), ((), ())), preferred_element_type=F32)


def dot_nt(a, b):
    return lax.dot_general(a, b, (((1,), (1,)), ((), ())), preferred_element_type=F32)


def dot_tn(a, b):
    return lax.dot_general(a, b, (((0,), (0,)), ((), ())), preferred_element_type=F32)


def key_bias(valid_ref, rows, padded):
    image, text = rows
    column = lax.broadcasted_iota(jnp.int32, (1, padded), 1)
    first = 2 * image
    second = first + text
    real = (column < first + valid_ref[0]) | ((column >= second) & (column < second + valid_ref[1]))
    return jnp.where(real, 0.0, NEGATIVE)


def pieces_of(rows):
    image, text = rows
    return ((0, image), (image, image), (2 * image, text), (2 * image + text, text))


def attend_kernel(rows, heads, padded, valid_ref, *refs):
    qkv, contexts, lse_ref, joint = (refs[:4], refs[4:8], refs[8], refs[9])
    width = heads * HD
    pieces = pieces_of(rows)
    total = 2 * sum(rows)
    for ref, (offset, size) in zip(qkv, pieces):
        joint[offset : offset + size, :] = ref[:, : 3 * width]
    if padded > total:
        joint[total:, :] = jnp.zeros((padded - total, 3 * width), BF16)
    bias = key_bias(valid_ref, rows, padded)
    for out in contexts:
        out[:, : 3 * width] = jnp.zeros((out.shape[0], 3 * width), BF16)
    for head in range(heads):
        at = head * HD
        keys = joint[:, width + at : width + at + HD]
        values = joint[:, 2 * width + at : 2 * width + at + HD]
        for ref, out, (offset, size) in zip(qkv, contexts, pieces):
            scores = dot_nt(ref[:, at : at + HD], keys) * score_scale + bias
            highest = jnp.max(scores, axis=-1, keepdims=True)
            weights = jnp.exp(scores - highest)
            totals = jnp.sum(weights, axis=-1, keepdims=True)
            probs = (weights * (1.0 / totals)).astype(BF16)
            out[:, 3 * width + at : 3 * width + at + HD] = dot_nn(probs, values).astype(BF16)
            lse_ref[offset : offset + size, head : head + 1] = highest + jnp.log(totals)


def attend_back_kernel(rows, heads, padded, valid_ref, *refs):
    qkv, contexts, grads, lse_ref = (refs[:4], refs[4:8], refs[8:12], refs[12])
    outs, joint, key_sum, value_sum = (refs[13:17], refs[17], refs[18], refs[19])
    width = heads * HD
    pieces = pieces_of(rows)
    total = 2 * sum(rows)
    for ref, (offset, size) in zip(qkv, pieces):
        joint[offset : offset + size, :] = ref[:, : 3 * width]
    if padded > total:
        joint[total:, :] = jnp.zeros((padded - total, 3 * width), BF16)
    for out in outs:
        out[:, 3 * width :] = jnp.zeros((out.shape[0], width), BF16)
    bias = key_bias(valid_ref, rows, padded)
    for head in range(heads):
        at = head * HD
        keys = joint[:, width + at : width + at + HD]
        values = joint[:, 2 * width + at : 2 * width + at + HD]
        for number, (offset, size) in enumerate(pieces):
            queries = qkv[number][:, at : at + HD]
            grad_context = grads[number][:, 3 * width + at : 3 * width + at + HD]
            context = contexts[number][:, 3 * width + at : 3 * width + at + HD]
            scores = dot_nt(queries, keys) * score_scale + bias
            probs = jnp.exp(scores - lse_ref[offset : offset + size, head : head + 1])
            grad_probs = dot_nt(grad_context, values)
            row_dots = jnp.sum(
                grad_context.astype(F32) * context.astype(F32), axis=-1, keepdims=True
            )
            grad_scores = (probs * (grad_probs - row_dots) * score_scale).astype(BF16)
            outs[number][:, at : at + HD] = dot_nn(grad_scores, keys).astype(BF16)
            value_part = dot_tn(probs.astype(BF16), grad_context)
            key_part = dot_tn(grad_scores, queries)
            if number == 0:
                value_sum[...] = value_part
                key_sum[...] = key_part
            else:
                value_sum[...] += value_part
                key_sum[...] += key_part
        for number, (offset, size) in enumerate(pieces):
            outs[number][:, width + at : width + at + HD] = key_sum[
                offset : offset + size, :
            ].astype(BF16)
            outs[number][:, 2 * width + at : 2 * width + at + HD] = value_sum[
                offset : offset + size, :
            ].astype(BF16)


def piece_specs(rows, columns):
    image, text = rows
    return [pl.BlockSpec((size, columns), lambda s, v: (s, 0)) for size in (image, image, text, text)]


def attend(rows, heads, seqs, valid, qkv):
    total = 2 * sum(rows)
    padded = -(-total // LANES) * LANES
    width = heads * HD
    sizes = (rows[0], rows[0], rows[1], rows[1])
    return pl.pallas_call(
        functools.partial(attend_kernel, rows, heads, padded),
        grid_spec=pltpu.PrefetchScalarGridSpec(
            num_scalar_prefetch=1,
            grid=(seqs,),
            in_specs=piece_specs(rows, qkv[0].shape[1]),
            out_specs=piece_specs(rows, 4 * width)
            + [pl.BlockSpec((None, total, LANES), lambda s, v: (s, 0, 0))],
            scratch_shapes=[pltpu.VMEM((padded, 3 * width), BF16)],
        ),
        out_shape=[jax.ShapeDtypeStruct((seqs * size, 4 * width), BF16) for size in sizes]
        + [jax.ShapeDtypeStruct((seqs, total, LANES), F32)],
        cost_estimate=pl.CostEstimate(
            flops=4 * seqs * heads * total * total * HD,
            bytes_accessed=8 * seqs * total * width,
            transcendentals=seqs * heads * total * total,
        ),
        name="attend",
    )(valid, *qkv)


def attend_back(rows, heads, seqs, valid, qkv, contexts, grads, lse):
    total = 2 * sum(rows)
    padded = -(-total // LANES) * LANES
    width = heads * HD
    sizes = (rows[0], rows[0], rows[1], rows[1])
    return pl.pallas_call(
        functools.partial(attend_back_kernel, rows, heads, padded),
        grid_spec=pltpu.PrefetchScalarGridSpec(
            num_scalar_prefetch=1,
            grid=(seqs,),
            in_specs=piece_specs(rows, qkv[0].shape[1])
            + piece_specs(rows, 4 * width)
            + piece_specs(rows, 4 * width)
            + [pl.BlockSpec((None, total, LANES), lambda s, v: (s, 0, 0))],
            out_specs=piece_specs(rows, 4 * width),
            scratch_shapes=[
                pltpu.VMEM((padded, 3 * width), BF16),
                pltpu.VMEM((padded, HD), F32),
                pltpu.VMEM((padded, HD), F32),
            ],
        ),
        out_shape=[jax.ShapeDtypeStruct((seqs * size, 4 * width), BF16) for size in sizes],
        cost_estimate=pl.CostEstimate(
            flops=10 * seqs * heads * total * total * HD,
            bytes_accessed=20 * seqs * total * width,
            transcendentals=seqs * heads * total * total,
        ),
        name="attend_back",
    )(valid, *qkv, *contexts, *grads, lse)


def swap_core(values):
    return lax.ppermute(values, "tensor", [(0, 1), (1, 0)])


def hop(values, distance, count):
    return lax.ppermute(values, "inner", [(i, i ^ distance) for i in range(count)])


def start_rows(rows, count):
    return [rows] + [hop(rows, j, count) for j in range(1, count)]


def finish_rows(blocks):
    own = jnp.concatenate(blocks, axis=0)
    return (own, swap_core(own))


def gather_rows(rows, count):
    return finish_rows(start_rows(rows, count))


def finish_both(blocks, image):
    return [
        finish_rows([block[part] for block in blocks])
        for part in (slice(image), slice(image, None))
    ]


def send_rows(own, other, count):
    arrived = swap_core(other.astype(BF16))
    blocks = (own + arrived.astype(F32)).reshape(count, own.shape[0] // count, own.shape[1])
    low = blocks.astype(BF16)
    return (blocks[0], [hop(low[j], j, count) for j in range(1, count)])


def add_rows(sent):
    total, parts = sent
    for part in parts:
        total = total + part.astype(F32)
    return total


def send_both(partials, count):
    arrived = swap_core(jnp.concatenate([p[1].astype(BF16) for p in partials], axis=0))
    middle = partials[0][0].shape[0]
    sums = [
        (p[0] + part.astype(F32)).reshape(count, p[0].shape[0] // count, p[0].shape[1])
        for p, part in zip(partials, (arrived[:middle], arrived[middle:]))
    ]
    lows = [
        jnp.concatenate([part[j].astype(BF16) for part in sums], axis=0)
        for j in range(1, count)
    ]
    return ([part[0] for part in sums], [hop(lows[j - 1], j, count) for j in range(1, count)])


def by_place(me_ref, count, body):
    for number in range(count):
        pl.when(me_ref[0] == number)(functools.partial(body, number))


def pack_attn_kernel(count, me_ref, qkv_ref, proj_ref, *outs):
    columns = proj_ref.shape[2] // count

    def place(number):
        for j, out in enumerate(outs):
            at = (j ^ number) * columns
            for n in range(2):
                base = 4 * n * columns
                for k in range(3):
                    out[:, base + k * columns : base + (k + 1) * columns] = qkv_ref[
                        n, k, :, at : at + columns
                    ].astype(BF16)
                out[:, base + 3 * columns : base + 4 * columns] = proj_ref[
                    n, :, at : at + columns
                ].astype(BF16)

    by_place(me_ref, count, place)


def pack_attn(me, qkv, proj, count):
    slab, full = proj.shape[1:]
    shape = jax.ShapeDtypeStruct((slab, 8 * full // count), BF16)
    return pl.pallas_call(
        functools.partial(pack_attn_kernel, count),
        grid_spec=pltpu.PrefetchScalarGridSpec(
            num_scalar_prefetch=1,
            grid=(1,),
            in_specs=[
                pl.BlockSpec(qkv.shape, lambda i, m: (0, 0, 0, 0)),
                pl.BlockSpec(proj.shape, lambda i, m: (0, 0, 0)),
            ],
            out_specs=[pl.BlockSpec(shape.shape, lambda i, m: (0, 0))] * count,
        ),
        out_shape=[shape] * count,
    )(me, qkv, proj)


def pack_ff_kernel(count, me_ref, up_ref, down_ref, *outs):
    columns = up_ref.shape[1] // count

    def place(number):
        for j, out in enumerate(outs):
            at = (j ^ number) * columns
            out[:, :columns] = up_ref[:, at : at + columns].astype(BF16)
            out[:, columns:] = down_ref[:, at : at + columns].astype(BF16)

    by_place(me_ref, count, place)


def pack_ff(me, up, down, n, count):
    slab, full = up.shape[1:]
    shape = jax.ShapeDtypeStruct((slab, 2 * full // count), BF16)
    spec = pl.BlockSpec((None, slab, full), lambda i, m: (n, 0, 0))
    return pl.pallas_call(
        functools.partial(pack_ff_kernel, count),
        grid_spec=pltpu.PrefetchScalarGridSpec(
            num_scalar_prefetch=1,
            grid=(1,),
            in_specs=[spec, spec],
            out_specs=[pl.BlockSpec(shape.shape, lambda i, m: (0, 0))] * count,
        ),
        out_shape=[shape] * count,
    )(me, up, down)


def unpack_kernel(count, me_ref, *refs):
    blocks, out = (refs[:count], refs[count])
    slab = blocks[0].shape[0]

    def place(number):
        for j, block in enumerate(blocks):
            at = (j ^ number) * slab
            out[at : at + slab, :] = block[...]

    by_place(me_ref, count, place)


def unpack(me, blocks):
    count = len(blocks)
    slab, columns = blocks[0].shape
    return pl.pallas_call(
        functools.partial(unpack_kernel, count),
        grid_spec=pltpu.PrefetchScalarGridSpec(
            num_scalar_prefetch=1,
            grid=(1,),
            in_specs=[pl.BlockSpec((slab, columns), lambda i, m: (0, 0))] * count,
            out_specs=pl.BlockSpec((count * slab, columns), lambda i, m: (0, 0)),
        ),
        out_shape=jax.ShapeDtypeStruct((count * slab, columns), BF16),
    )(me, *blocks)


def merge_kernel(count, me_ref, own_ref, others_ref, out):
    slab = own_ref.shape[0]

    def place(number):
        for j in range(count):
            at = (j ^ number) * slab
            if j == 0:
                out[at : at + slab, :] = own_ref[...]
            else:
                out[at : at + slab, :] = others_ref[(j - 1) * slab : j * slab, :]

    by_place(me_ref, count, place)


def merge(me, own, others, slab, count):
    columns = own.shape[1]
    outer = own.shape[0] // slab
    return pl.pallas_call(
        functools.partial(merge_kernel, count),
        grid_spec=pltpu.PrefetchScalarGridSpec(
            num_scalar_prefetch=1,
            grid=(outer,),
            in_specs=[
                pl.BlockSpec((slab, columns), lambda i, m: (i, 0)),
                pl.BlockSpec(((count - 1) * slab, columns), lambda i, m: (i, 0)),
            ],
            out_specs=pl.BlockSpec((count * slab, columns), lambda i, m: (i, 0)),
        ),
        out_shape=jax.ShapeDtypeStruct((outer * count * slab, columns), BF16),
    )(me, own, others)


def adam_refs(gradient, weight, mean, second, outs):
    updated, mean_new, second_new = adam_step(weight, gradient, mean, second)
    for out, value in zip(outs, (gradient, updated, mean_new, second_new)):
        out[...] = value


def adam_ff_kernel(count, me_ref, *refs):
    blocks, (weight, mean, second) = (refs[:count], refs[count : count + 3])
    outs, gradient = (refs[-5:-1], refs[-1])
    wanted = pl.program_id(0) ^ me_ref[0]
    for j, block in enumerate(blocks):

        @pl.when(wanted == j)
        def take(block=block):
            gradient[...] = block[...].astype(F32)

    adam_refs(gradient[...], weight[...], mean[...], second[...], outs)


def adam_ff(me, blocks, half, weight, mean, second, n, before):
    count = len(blocks)
    slab, columns = (blocks[0].shape[0], blocks[0].shape[1] // 2)
    spec = pl.BlockSpec((None, slab, columns), lambda c, m: (n, 0, c))
    return pl.pallas_call(
        functools.partial(adam_ff_kernel, count),
        grid_spec=pltpu.PrefetchScalarGridSpec(
            num_scalar_prefetch=1,
            grid=(count,),
            in_specs=[pl.BlockSpec((slab, columns), lambda c, m: (0, half))] * count
            + [spec] * 3
            + [pl.BlockSpec(memory_space=pl.ANY)] * len(before),
            out_specs=[spec] * 4,
            scratch_shapes=[pltpu.VMEM((slab, columns), F32)],
        ),
        out_shape=[jax.ShapeDtypeStruct(weight.shape, F32)] * 4,
        input_output_aliases={1 + count + 3 + i: i for i in range(len(before))},
    )(me, *blocks, weight, mean, second, *before)


def adam_attn_kernel(count, parts, me_ref, *refs):
    blocks, (weight, mean, second) = (refs[:count], refs[count : count + 3])
    outs, gradient = (refs[-5:-1], refs[-1])
    columns = gradient.shape[1] // count
    step = pl.program_id(0)

    def place(number):
        for k in range(parts):

            @pl.when(step == k)
            def take(k=k):
                for j, block in enumerate(blocks):
                    at = (j ^ number) * columns
                    gradient[:, at : at + columns] = block[
                        :, k * columns : (k + 1) * columns
                    ].astype(F32)

    by_place(me_ref, count, place)
    adam_refs(gradient[...], weight[...], mean[...], second[...], outs)


def adam_attn(me, count, blocks, weight, mean, second):
    parts, slab, full = weight.shape
    size = blocks[0].shape[1] * len(blocks) // count
    places = [j if len(blocks) == 1 else 0 for j in range(count)]
    blocks = blocks * (count // len(blocks))
    spec = pl.BlockSpec((None, slab, full), lambda k, m: (k, 0, 0))
    return pl.pallas_call(
        functools.partial(adam_attn_kernel, count, parts),
        grid_spec=pltpu.PrefetchScalarGridSpec(
            num_scalar_prefetch=1,
            grid=(parts,),
            in_specs=[
                pl.BlockSpec((slab, size), functools.partial(lambda at, k, m: (0, at), at))
                for at in places
            ]
            + [spec] * 3,
            out_specs=[spec] * 4,
            scratch_shapes=[pltpu.VMEM((slab, full), F32)],
        ),
        out_shape=[jax.ShapeDtypeStruct(weight.shape, F32)] * 4,
    )(me, *blocks, weight, mean, second)


def exchange(blocks, count):
    return [blocks[0]] + [hop(blocks[j], j, count) for j in range(1, count)]


def after(values, *done):
    return jax.tree.map(lambda value: lax.optimization_barrier((value, done))[0], values)


def whole(array):
    return pl.BlockSpec(array.shape, lambda i, m: (0,) * len(array.shape))


def row_kernel(body, place, inputs, outputs, scratch=()):
    return pl.pallas_call(
        body,
        grid_spec=pltpu.PrefetchScalarGridSpec(
            num_scalar_prefetch=1,
            grid=(1,),
            in_specs=[whole(a) for a in inputs],
            out_specs=[whole(a) for a in outputs],
            scratch_shapes=list(scratch),
        ),
        out_shape=list(outputs),
    )(place, *inputs)


def fold(values):
    return jnp.sum(values.reshape(values.shape[0] // 8, 8, values.shape[1]), axis=0)


def arrived_rows(own, parts, where, offset):
    total = own[where, :]
    for part in parts:
        total = total + part[pl.ds(pl.multiple_of(offset, CHUNK), CHUNK), :].astype(F32)
    return total


def middle_back_kernel(n, me_ref, own, *refs):
    parts, (middle, attn, cotangent, mods) = (refs[:-7], refs[-7:-3])
    grad_out, low_out, sums_out = refs[-3:]
    zero = jnp.zeros((8, own.shape[1]), F32)
    scale, gate = (mods[n, 4:5, :], mods[n, 2:3, :])

    def step(i, sums):
        where = pl.ds(pl.multiple_of(i * CHUNK, CHUNK), CHUNK)
        grad = arrived_rows(own, parts, where, i * CHUNK)
        normed, inv_std = layer_norm(middle[where, :])
        total = cotangent[where, :].astype(F32) + norm_back(grad * (1.0 + scale), normed, inv_std)
        grad_out[where, :] = total
        low_out[where, :] = (total * gate).astype(BF16)
        terms = (total * attn[where, :], grad, grad * normed)
        return tuple(a + fold(b) for a, b in zip(sums, terms))

    sums = lax.fori_loop(0, own.shape[0] // CHUNK, step, (zero,) * 3)
    for k, value in enumerate(sums):
        sums_out[k : k + 1, :] = jnp.sum(value, axis=0, keepdims=True)


def middle_back(place, n, sent, middle, attn, cotangent, mods):
    own, parts = sent
    return row_kernel(
        functools.partial(middle_back_kernel, n),
        place,
        (own, *parts, middle, attn, cotangent, mods),
        (
            jax.ShapeDtypeStruct(own.shape, F32),
            jax.ShapeDtypeStruct(own.shape, BF16),
            jax.ShapeDtypeStruct((8, own.shape[1]), F32),
        ),
    )


def end_kernel(arrivals, me_ref, *refs):
    mods, back = (refs[0], refs[1 : 1 + arrivals])
    streams = refs[1 + arrivals : -4]
    each = len(streams) // 2
    grads_out, rows_out, owners_out, table = refs[-4:]
    offset = 0
    for n in range(2):
        own, tokens, grad_middle, cotangent, middle, sums, down = streams[n * each :][:7]
        parts = streams[n * each + 7 : (n + 1) * each]
        zero = jnp.zeros((8, own.shape[1]), F32)
        scale, gate = (mods[n, 1:2, :], mods[n, 5:6, :])

        def step(i, totals):
            where = pl.ds(pl.multiple_of(i * CHUNK, CHUNK), CHUNK)
            place = pl.ds(pl.multiple_of(offset + i * CHUNK, CHUNK), CHUNK)
            grad = arrived_rows(own, back, where, offset + i * CHUNK)
            normed, inv_std = layer_norm(tokens[where, :].astype(F32))
            grads_out[place, :] = grad_middle[where, :] + norm_back(
                grad * (1.0 + scale), normed, inv_std
            )
            total = arrived_rows(down, parts, where, i * CHUNK)
            rows_out[place, :] = middle[where, :] + gate * total
            terms = (grad, grad * normed, cotangent[where, :].astype(F32) * total)
            return tuple(a + fold(b) for a, b in zip(totals, terms))

        totals = lax.fori_loop(0, own.shape[0] // CHUNK, step, (zero,) * 3)
        for k, value in zip((0, 1, 5), totals):
            table[6 * n + k : 6 * n + k + 1, :] = jnp.sum(value, axis=0, keepdims=True)
        table[6 * n + 2 : 6 * n + 5, :] = sums[0:3, :]
        offset += own.shape[0]
    width = table.shape[1]
    devices, _, columns = owners_out.shape
    for n in range(2):
        for d in range(devices):
            done = 0
            while done < columns:
                k, at = divmod(d * columns + done, width)
                size = min(columns - done, width - at)
                owners_out[d, n : n + 1, done : done + size] = table[
                    6 * n + k : 6 * n + k + 1, at : at + size
                ]
                done += size


def end_rows(place, mods, sent_one, streams, down_sent, devices):
    owns, back = sent_one
    inputs = [mods, *back]
    for n in range(2):
        inputs += [owns[n], *streams[n], down_sent[n][0], *down_sent[n][1]]
    rows, width = back[0].shape
    columns = 6 * width // devices
    return row_kernel(
        functools.partial(end_kernel, len(back)),
        place,
        inputs,
        (
            jax.ShapeDtypeStruct((rows, width), F32),
            jax.ShapeDtypeStruct((rows, width), F32),
            jax.ShapeDtypeStruct((devices, 2, columns), F32),
        ),
        (pltpu.VMEM((16, width), F32),),
    )


def whole_rows_kernel(core_ref, own, other, *outs):
    for core in range(2):

        @pl.when(core_ref[0] == core)
        def place(core=core):
            start = 0
            for out in outs:
                length = out.shape[1]
                size = (own.shape[0] - start) if start else length // 2
                for number, source in ((core, own), (1 - core, other)):
                    count = min(size, length - number * size)
                    out[0, number * size : number * size + count, :] = source[
                        start : start + count, :
                    ]
                start += size


def whole_rows(core, own, lengths):
    return row_kernel(
        whole_rows_kernel,
        core,
        (own, swap_core(own)),
        [jax.ShapeDtypeStruct((1, length, own.shape[1]), F32) for length in lengths],
    )


def attn_gradient_kernel(columns, me_ref, *refs):
    shifted, grads, proj_ins, contexts = (refs[:2], refs[2:4], refs[4:6], refs[6:8])
    qkv_out, proj_out = refs[8:]
    full = grads[0].shape[1]
    split = columns // 256 * 256
    for low, high in ((0, split), (split, full)):
        total = None
        terms = list(zip(shifted, grads))
        if high > columns:
            terms += list(zip(proj_ins, contexts))
        for left, right in terms:
            part = dot_tn(left[...], right[:, low:high])
            total = part if total is None else total + part
        total = total.astype(BF16)
        if high > columns:
            qkv_out[:, low:] = total[:, : columns - low]
            proj_out[...] = total[:, columns - low :]
        else:
            qkv_out[:, low:high] = total


def attn_gradient(place, columns, shifted, grads, proj_ins, contexts):
    width = shifted[0].shape[1]
    full = grads[0].shape[1]
    tile = math.gcd(512, width)
    left = [pl.BlockSpec((a.shape[0], tile), lambda i, m: (0, i)) for a in shifted]
    right = [pl.BlockSpec(a.shape, lambda i, m: (0, 0)) for a in grads]
    rows = shifted[0].shape[0]
    return pl.pallas_call(
        functools.partial(attn_gradient_kernel, columns),
        grid_spec=pltpu.PrefetchScalarGridSpec(
            num_scalar_prefetch=1,
            grid=(width // tile,),
            in_specs=(left + right) * 2,
            out_specs=[
                pl.BlockSpec((tile, size), lambda i, m: (i, 0)) for size in (columns, full - columns)
            ],
        ),
        out_shape=[jax.ShapeDtypeStruct((width, size), BF16) for size in (columns, full - columns)],
        cost_estimate=pl.CostEstimate(
            flops=4 * rows * width * full, bytes_accessed=8 * rows * width, transcendentals=0
        ),
    )(place, *shifted, *grads, *proj_ins, *contexts)


def local(
    image_tokens,
    text_tokens,
    image_cotangent,
    text_cotangent,
    timesteps,
    mod_weight,
    mod_bias,
    qkv_weight,
    proj_weight,
    up_weight,
    down_weight,
    mean_mod,
    second_mod,
    mean_bias,
    second_bias,
    mean_qkv,
    second_qkv,
    mean_proj,
    second_proj,
    mean_up,
    second_up,
    mean_down,
    second_down,
):
    count = lax.axis_size("inner")
    cores = lax.axis_size("tensor")
    me = lax.axis_index("inner")
    core = lax.axis_index("tensor")
    every = ("outer", "inner", "tensor")
    streams = (0, 1)
    seq_count = timesteps.shape[0]
    devices = seq_count * cores
    column_count = mod_weight.shape[2]
    width = image_tokens.shape[2]
    slab = qkv_weight.shape[1]
    head_cols = qkv_weight.shape[3] // count
    heads = head_cols // HD
    unit_cols = up_weight.shape[2] // count
    lengths = (image_tokens.shape[1], text_tokens.shape[1])
    rows = tuple(-(-length // (16 * cores)) * 16 for length in lengths)

    place = me.astype(jnp.int32)[None]
    qkv_all = [a.transpose(0, 2, 1, 3) for a in (qkv_weight, mean_qkv, second_qkv)]
    proj_all = [a.transpose(0, 2, 1) for a in (proj_weight, mean_proj, second_proj)]
    up_all = (up_weight, mean_up, second_up)
    down_all = [a.transpose(0, 2, 1) for a in (down_weight, mean_down, second_down)]

    def full_weight(shard):
        return lax.all_gather(shard, "outer", axis=0, tiled=True)

    blocks = pack_attn(place, qkv_all[0], proj_all[0], count)
    own_full = full_weight(blocks[0])
    shard = jnp.concatenate(exchange(blocks, count)[1:], axis=0)
    attn_both = merge(place, own_full, full_weight(shard), slab, count)

    half_width = width // 2
    frequency = jnp.exp(-math.log(10000.0) * jnp.arange(half_width, dtype=F32) / half_width)
    angles = timesteps.astype(F32)[:, None] * frequency[None, :]
    all_cond = jax.nn.silu(jnp.concatenate([jnp.cos(angles), jnp.sin(angles)], axis=1)).astype(BF16)
    bias_low = lax.optimization_barrier(mod_bias.astype(BF16)).astype(F32)
    local_mod = (
        jnp.einsum("sd,ndc->snc", all_cond, mod_weight.astype(BF16), preferred_element_type=F32)
        + bias_low[None, :, :]
    )
    to_cores = jnp.broadcast_to(
        local_mod[:, None], (seq_count, cores, 2, column_count)
    ).reshape(devices, 2, column_count)
    spread = lax.all_to_all(to_cores, every, split_axis=0, concat_axis=0, tiled=True)
    mods = after(spread, shard).transpose(1, 0, 2).reshape(2, 6, width)

    def own_rows(tokens, size):
        short = cores * size - tokens.shape[1]
        padded = jnp.pad(tokens[0], ((0, short), (0, 0)))
        return lax.dynamic_slice(padded, (core * size, 0), (size, width))

    tokens = [own_rows(t, r) for t, r in zip((image_tokens, text_tokens), rows)]
    inputs = [t.astype(F32) for t in tokens]
    cotangents = [own_rows(t, r) for t, r in zip((image_cotangent, text_cotangent), rows)]
    valid = jnp.stack(
        [
            jnp.clip(lengths[1] - core * rows[1], 0, rows[1]),
            jnp.clip(lengths[1] - (1 - core) * rows[1], 0, rows[1]),
        ]
    ).astype(jnp.int32)

    shifted_one = []
    for n in streams:
        normed, _ = layer_norm(inputs[n])
        shifted_one.append((normed * (1.0 + mods[n, 1]) + mods[n, 0]).astype(BF16))
    shifted_one = finish_both(start_rows(jnp.concatenate(shifted_one, axis=0), count), rows[0])

    def ff_blocks(n, where):
        return exchange(pack_ff(where, up_all[0], down_all[0], n, count), count)

    shard = unpack(place, ff_blocks(0, after(place, shifted_one)))
    ff_full = [full_weight(shard)]
    blocks = ff_blocks(1, after(place, shard))
    gated = [
        (after(cotangents[n], shard).astype(F32) * mods[n, 5]).astype(BF16) for n in streams
    ]
    gated = start_rows(jnp.concatenate(gated, axis=0), count)

    wide = 4 * head_cols
    attn_full = [attn_both[:, :wide], attn_both[:, wide:]]
    qkv_pieces = [
        dot_nn(half, attn_full[n]).astype(BF16) for n in streams for half in shifted_one[n]
    ]
    *context_pieces, lse = attend(rows, heads, count, valid, qkv_pieces)
    contexts = (context_pieces[:2], context_pieces[2:])
    ff_full.append(full_weight(unpack(place, after(blocks, context_pieces))))
    attn_sums, middles, shifted_two, middle_rows = ([], [], [], [])
    for n in streams:
        partial = [dot_nt(half, attn_full[n]) for half in contexts[n]]
        attn_sum = add_rows(send_rows(partial[0], partial[1], count))
        middle = inputs[n] + mods[n, 2] * attn_sum
        normed, _ = layer_norm(middle)
        shifted = (normed * (1.0 + mods[n, 4]) + mods[n, 3]).astype(BF16)
        attn_sums.append(attn_sum)
        middles.append(middle)
        middle_rows.append(shifted)
        shifted_two.append(gather_rows(shifted, count))

    def outer_sum(gradient):
        return lax.psum_scatter(gradient, "outer", scatter_dimension=0, tiled=True)

    def owned(summed):
        return exchange(
            [
                lax.dynamic_slice(summed, ((me ^ j) * slab, 0), (slab, summed.shape[1]))
                for j in range(count)
            ],
            count,
        )

    down_ins = finish_both(after(gated, middle_rows[0]), rows[0])
    ff_full[0] = after(ff_full[0], middle_rows[0])
    grad_contexts, grad_middles, partial_rows, proj_ins = ([], [], [], [])
    ff_sums = []
    for n in streams:
        full = ff_full[n] if n == 0 else after(ff_full[n], proj_in, down_partials)
        up_full, down_full = (full[:, :unit_cols], full[:, unit_cols:])
        pairs = [gelu_pair(dot_nn(half, up_full)) for half in shifted_two[n]]
        hidden = [pair[0].astype(BF16) for pair in pairs]

        def down_gradient(where):
            total = dot_tn(where[0], hidden[0]) + dot_tn(where[1], hidden[1])
            return total.astype(BF16)

        grad_ins = down_ins[n]
        if n == 1:
            grad_down = down_gradient(grad_ins)
            grad_ins = after(grad_ins, grad_down)
        grad_pres = [
            (dot_nn(down_in, down_full) * pair[1]).astype(BF16)
            for down_in, pair in zip(grad_ins, pairs)
        ]
        partial = [dot_nt(grad_pre, up_full) for grad_pre in grad_pres]
        sent = send_rows(partial[0], partial[1], count)
        if n == 0:
            grad_down = down_gradient(after(grad_ins, partial))
            partial = (partial, grad_down)
        grad_pres = after(grad_pres, partial)
        total = dot_tn(shifted_two[n][0], grad_pres[0]) + dot_tn(shifted_two[n][1], grad_pres[1])
        grad_up = total.astype(BF16)
        ff_sums.append(outer_sum(jnp.concatenate([grad_down, grad_up], axis=1)))
        grad_middle, proj_in, sums = middle_back(
            place, n, after(sent, grad_up), middles[n], attn_sums[n], cotangents[n], mods
        )
        halves = gather_rows(proj_in, count)
        grad_contexts += [dot_nn(half, attn_full[n]).astype(BF16) for half in halves]
        proj_ins.append(halves)
        grad_middles.append(grad_middle)
        partial_rows.append(sums)
        if n == 0:
            down_partials = [dot_nt(half, down_full) for half in after(hidden, proj_in)]
    down_sent = send_rows(down_partials[0], down_partials[1], count)
    ff_sums[0] = after(ff_sums[0], grad_contexts)

    grad_pieces = attend_back(
        rows, heads, count, valid, qkv_pieces, context_pieces, grad_contexts, lse
    )
    grad_qkv_rows = (grad_pieces[:2], grad_pieces[2:])
    grad_attn = []
    for n in streams:
        grad_attn.append(
            attn_gradient(
                place, 3 * head_cols, shifted_one[n], grad_qkv_rows[n], proj_ins[n], contexts[n]
            )
        )
    qkv_sum = outer_sum(jnp.concatenate([pair[0] for pair in grad_attn], axis=1))
    proj_both = jnp.concatenate([pair[1] for pair in grad_attn], axis=1)
    proj_both = proj_both.reshape(-1, count, slab, proj_both.shape[1])
    grad_qkv_rows = after(grad_qkv_rows, grad_attn)
    partials = [[dot_nt(half, attn_full[n]) for half in grad_qkv_rows[n]] for n in streams]
    sent_one = send_both(partials, count)
    hidden, down_sent = after((hidden, down_sent), partials)
    down_partials = [dot_nt(half, down_full) for half in hidden]
    down_sent = [down_sent, send_rows(down_partials[0], down_partials[1], count)]

    def adam_both(n, before):
        blocks = owned(ff_sums[n])
        return [
            adam_ff(place, blocks, half, *arrays, n, outs)
            for half, arrays, outs in zip((0, 1), (down_all, up_all), before)
        ]

    ff_outs = adam_both(0, ((), ()))
    grad_rows, out_rows, to_owners = end_rows(
        place,
        mods,
        after(sent_one, down_partials, ff_outs[0][0], ff_outs[1][0]),
        [
            (tokens[n], grad_middles[n], cotangents[n], middles[n], partial_rows[n])
            for n in streams
        ],
        down_sent,
        devices,
    )

    blocks = exchange(
        [
            lax.dynamic_index_in_dim(proj_both, me ^ j, axis=1, keepdims=False)
            for j in range(count)
        ],
        count,
    )
    blocks = after(blocks, to_owners)
    proj_sum = outer_sum(jnp.concatenate(blocks, axis=2).reshape(-1, count * proj_both.shape[3]))

    received = lax.all_to_all(to_owners, every, split_axis=0, concat_axis=0, tiled=True)
    own_columns = received.reshape(seq_count, cores, 2, column_count).sum(axis=1)
    grad_mod = jnp.einsum(
        "sd,snc->ndc", all_cond.astype(F32), own_columns, precision=lax.Precision.HIGHEST
    )
    grad_bias = jnp.sum(own_columns, axis=0)
    new_mod, mean_mod_next, second_mod_next = adam_step(mod_weight, grad_mod, mean_mod, second_mod)
    new_bias, mean_bias_next, second_bias_next = adam_step(
        mod_bias, grad_bias, mean_bias, second_bias
    )

    core_place = core.astype(jnp.int32)[None]
    image_out, text_out = whole_rows(core_place, out_rows, lengths)
    image_grad, text_grad = whole_rows(core_place, grad_rows, lengths)

    ff_sums[1] = after(ff_sums[1], to_owners)
    ff_outs = adam_both(1, ff_outs)
    down_outs, up_outs = ff_outs
    qkv_outs = adam_attn(
        place,
        count,
        owned(after(qkv_sum, new_mod, text_out, text_grad)),
        *(a.reshape(6, *a.shape[2:]) for a in qkv_all),
    )
    proj_outs = adam_attn(
        place, count, [after(proj_sum, qkv_outs[0], up_outs[0], down_outs[0])], *proj_all
    )
    grad_up, new_up, mean_up_next, second_up_next = up_outs
    grad_down, new_down, mean_down_next, second_down_next = (
        a.transpose(0, 2, 1) for a in down_outs
    )
    grad_qkv, new_qkv, mean_qkv_next, second_qkv_next = (
        a.reshape(qkv_all[0].shape).transpose(0, 2, 1, 3) for a in qkv_outs
    )
    grad_proj, new_proj, mean_proj_next, second_proj_next = (
        a.transpose(0, 2, 1) for a in proj_outs
    )
    return (
        image_out,
        text_out,
        image_grad,
        text_grad,
        grad_mod,
        grad_bias,
        grad_qkv,
        grad_proj,
        grad_up,
        grad_down,
        new_mod,
        new_bias,
        new_qkv,
        new_proj,
        new_up,
        new_down,
        mean_mod_next,
        second_mod_next,
        mean_bias_next,
        second_bias_next,
        mean_qkv_next,
        second_qkv_next,
        mean_proj_next,
        second_proj_next,
        mean_up_next,
        second_up_next,
        mean_down_next,
        second_down_next,
    )


def solution(mesh):
    dp, cores = mesh.devices.shape
    inner = math.gcd(dp, INNER)
    split = Mesh(mesh.devices.reshape(dp // inner, inner, cores), ("outer", "inner", "tensor"))
    group = ("outer", "inner")
    every = ("outer", "inner", "tensor")
    tokens = P(group, None, None)
    mod, bias = (P(None, None, every), P(None, every))
    qkv = P(None, group, None, "tensor")
    columns = P(None, group, "tensor")
    rows = P(None, "tensor", group)
    return jax.shard_map(
        local,
        mesh=split,
        in_specs=(tokens,) * 4
        + (P(),)
        + (mod, bias, qkv, rows, columns, rows)
        + (mod, mod, bias, bias, qkv, qkv, rows, rows, columns, columns, rows, rows),
        out_specs=(tokens,) * 4
        + (mod, bias, qkv, rows, columns, rows)
        + (mod, bias, qkv, rows, columns, rows)
        + (mod, mod, bias, bias, qkv, qkv, rows, rows, columns, columns, rows, rows),
        check_vma=False,
    )
```

```python
import functools
import math

import jax
import jax.numpy as jnp
from jax import lax
from jax.experimental import pallas as pl
from jax.experimental.pallas import tpu as pltpu
from jax.sharding import Mesh
from jax.sharding import PartitionSpec as P


HD = 64
ADAM_STEP = 10
INNER = 4

eps_norm = 1e-06
beta_one = 0.9
beta_two = 0.999
adam_eps = 1e-08
learn_rate = 0.02
decay_rate = 0.1
gelu_coef = 0.7978845608028654
cubic_coef = 0.044715
score_scale = 1.0 / math.sqrt(HD)
NEGATIVE = -1e30
LANES = 128
CHUNK = 16

F32 = jnp.float32
BF16 = jnp.bfloat16


def layer_norm(values):
    average = jnp.mean(values, axis=-1, keepdims=True)
    centred = values - average
    variance = jnp.mean(centred * centred, axis=-1, keepdims=True)
    inv_std = lax.rsqrt(variance + eps_norm)
    return (centred * inv_std, inv_std)


def norm_back(grad_normed, normed, inv_std):
    mean_grad = jnp.mean(grad_normed, axis=-1, keepdims=True)
    mean_cross = jnp.mean(grad_normed * normed, axis=-1, keepdims=True)
    return inv_std * (grad_normed - mean_grad - normed * mean_cross)


def gelu_pair(inputs):
    argument = gelu_coef * (inputs + cubic_coef * inputs * inputs * inputs)
    tangent = jnp.tanh(argument)
    activated = 0.5 * inputs * (1.0 + tangent)
    derivative = 0.5 * (1.0 + tangent) + 0.5 * inputs * (1.0 - tangent * tangent) * gelu_coef * (
        1.0 + 3.0 * cubic_coef * inputs * inputs
    )
    return (activated, derivative)


def adam_step(weight, gradient, mean_old, second_old):
    mean_new = beta_one * mean_old + (1.0 - beta_one) * gradient
    second_new = beta_two * second_old + (1.0 - beta_two) * gradient * gradient
    mean_hat = mean_new / (1.0 - beta_one**ADAM_STEP)
    second_hat = second_new / (1.0 - beta_two**ADAM_STEP)
    updated = weight - learn_rate * (
        mean_hat / (jnp.sqrt(second_hat) + adam_eps) + decay_rate * weight
    )
    return (updated, mean_new, second_new)


def dot_nn(a, b):
    return lax.dot_general(a, b, (((1,), (0,)), ((), ())), preferred_element_type=F32)


def dot_nt(a, b):
    return lax.dot_general(a, b, (((1,), (1,)), ((), ())), preferred_element_type=F32)


def dot_tn(a, b):
    return lax.dot_general(a, b, (((0,), (0,)), ((), ())), preferred_element_type=F32)


def key_bias(valid_ref, rows, padded):
    image, text = rows
    column = lax.broadcasted_iota(jnp.int32, (1, padded), 1)
    first = 2 * image
    second = first + text
    real = (column < first + valid_ref[0]) | ((column >= second) & (column < second + valid_ref[1]))
    return jnp.where(real, 0.0, NEGATIVE)


def pieces_of(rows):
    image, text = rows
    return ((0, image), (image, image), (2 * image, text), (2 * image + text, text))


def attend_kernel(rows, heads, padded, valid_ref, *refs):
    qkv, contexts, lse_ref, joint = (refs[:4], refs[4:8], refs[8], refs[9])
    width = heads * HD
    pieces = pieces_of(rows)
    total = 2 * sum(rows)
    for ref, (offset, size) in zip(qkv, pieces):
        joint[offset : offset + size, :] = ref[:, : 3 * width]
    if padded > total:
        joint[total:, :] = jnp.zeros((padded - total, 3 * width), BF16)
    bias = key_bias(valid_ref, rows, padded)
    for out in contexts:
        out[:, : 3 * width] = jnp.zeros((out.shape[0], 3 * width), BF16)
    for head in range(heads):
        at = head * HD
        keys = joint[:, width + at : width + at + HD]
        values = joint[:, 2 * width + at : 2 * width + at + HD]
        for ref, out, (offset, size) in zip(qkv, contexts, pieces):
            scores = dot_nt(ref[:, at : at + HD], keys) * score_scale + bias
            highest = jnp.max(scores, axis=-1, keepdims=True)
            weights = jnp.exp(scores - highest)
            totals = jnp.sum(weights, axis=-1, keepdims=True)
            probs = (weights * (1.0 / totals)).astype(BF16)
            out[:, 3 * width + at : 3 * width + at + HD] = dot_nn(probs, values).astype(BF16)
            lse_ref[offset : offset + size, head : head + 1] = highest + jnp.log(totals)


def attend_back_kernel(rows, heads, padded, valid_ref, *refs):
    qkv, contexts, grads, lse_ref = (refs[:4], refs[4:8], refs[8:12], refs[12])
    outs, joint, key_sum, value_sum = (refs[13:17], refs[17], refs[18], refs[19])
    width = heads * HD
    pieces = pieces_of(rows)
    total = 2 * sum(rows)
    for ref, (offset, size) in zip(qkv, pieces):
        joint[offset : offset + size, :] = ref[:, : 3 * width]
    if padded > total:
        joint[total:, :] = jnp.zeros((padded - total, 3 * width), BF16)
    for out in outs:
        out[:, 3 * width :] = jnp.zeros((out.shape[0], width), BF16)
    bias = key_bias(valid_ref, rows, padded)
    for head in range(heads):
        at = head * HD
        keys = joint[:, width + at : width + at + HD]
        values = joint[:, 2 * width + at : 2 * width + at + HD]
        for number, (offset, size) in enumerate(pieces):
            queries = qkv[number][:, at : at + HD]
            grad_context = grads[number][:, 3 * width + at : 3 * width + at + HD]
            context = contexts[number][:, 3 * width + at : 3 * width + at + HD]
            scores = dot_nt(queries, keys) * score_scale + bias
            probs = jnp.exp(scores - lse_ref[offset : offset + size, head : head + 1])
            grad_probs = dot_nt(grad_context, values)
            row_dots = jnp.sum(
                grad_context.astype(F32) * context.astype(F32), axis=-1, keepdims=True
            )
            grad_scores = (probs * (grad_probs - row_dots) * score_scale).astype(BF16)
            outs[number][:, at : at + HD] = dot_nn(grad_scores, keys).astype(BF16)
            value_part = dot_tn(probs.astype(BF16), grad_context)
            key_part = dot_tn(grad_scores, queries)
            if number == 0:
                value_sum[...] = value_part
                key_sum[...] = key_part
            else:
                value_sum[...] += value_part
                key_sum[...] += key_part
        for number, (offset, size) in enumerate(pieces):
            outs[number][:, width + at : width + at + HD] = key_sum[
                offset : offset + size, :
            ].astype(BF16)
            outs[number][:, 2 * width + at : 2 * width + at + HD] = value_sum[
                offset : offset + size, :
            ].astype(BF16)


def piece_specs(rows, columns):
    image, text = rows
    return [pl.BlockSpec((size, columns), lambda s, v: (s, 0)) for size in (image, image, text, text)]


def attend(rows, heads, seqs, valid, qkv):
    total = 2 * sum(rows)
    padded = -(-total // LANES) * LANES
    width = heads * HD
    sizes = (rows[0], rows[0], rows[1], rows[1])
    return pl.pallas_call(
        functools.partial(attend_kernel, rows, heads, padded),
        grid_spec=pltpu.PrefetchScalarGridSpec(
            num_scalar_prefetch=1,
            grid=(seqs,),
            in_specs=piece_specs(rows, qkv[0].shape[1]),
            out_specs=piece_specs(rows, 4 * width)
            + [pl.BlockSpec((None, total, LANES), lambda s, v: (s, 0, 0))],
            scratch_shapes=[pltpu.VMEM((padded, 3 * width), BF16)],
        ),
        out_shape=[jax.ShapeDtypeStruct((seqs * size, 4 * width), BF16) for size in sizes]
        + [jax.ShapeDtypeStruct((seqs, total, LANES), F32)],
        cost_estimate=pl.CostEstimate(
            flops=4 * seqs * heads * total * total * HD,
            bytes_accessed=8 * seqs * total * width,
            transcendentals=seqs * heads * total * total,
        ),
        name="attend",
    )(valid, *qkv)


def attend_back(rows, heads, seqs, valid, qkv, contexts, grads, lse):
    total = 2 * sum(rows)
    padded = -(-total // LANES) * LANES
    width = heads * HD
    sizes = (rows[0], rows[0], rows[1], rows[1])
    return pl.pallas_call(
        functools.partial(attend_back_kernel, rows, heads, padded),
        grid_spec=pltpu.PrefetchScalarGridSpec(
            num_scalar_prefetch=1,
            grid=(seqs,),
            in_specs=piece_specs(rows, qkv[0].shape[1])
            + piece_specs(rows, 4 * width)
            + piece_specs(rows, 4 * width)
            + [pl.BlockSpec((None, total, LANES), lambda s, v: (s, 0, 0))],
            out_specs=piece_specs(rows, 4 * width),
            scratch_shapes=[
                pltpu.VMEM((padded, 3 * width), BF16),
                pltpu.VMEM((padded, HD), F32),
                pltpu.VMEM((padded, HD), F32),
            ],
        ),
        out_shape=[jax.ShapeDtypeStruct((seqs * size, 4 * width), BF16) for size in sizes],
        cost_estimate=pl.CostEstimate(
            flops=10 * seqs * heads * total * total * HD,
            bytes_accessed=20 * seqs * total * width,
            transcendentals=seqs * heads * total * total,
        ),
        name="attend_back",
    )(valid, *qkv, *contexts, *grads, lse)


def swap_core(values):
    return lax.ppermute(values, "tensor", [(0, 1), (1, 0)])


def hop(values, distance, count):
    return lax.ppermute(values, "inner", [(i, i ^ distance) for i in range(count)])


def start_rows(rows, count):
    return [rows] + [hop(rows, j, count) for j in range(1, count)]


def finish_rows(blocks):
    own = jnp.concatenate(blocks, axis=0)
    return (own, swap_core(own))


def gather_rows(rows, count):
    return finish_rows(start_rows(rows, count))


def finish_both(blocks, image):
    return [
        finish_rows([block[part] for block in blocks])
        for part in (slice(image), slice(image, None))
    ]


def send_rows(own, other, count):
    arrived = swap_core(other.astype(BF16))
    blocks = (own + arrived.astype(F32)).reshape(count, own.shape[0] // count, own.shape[1])
    low = blocks.astype(BF16)
    return (blocks[0], [hop(low[j], j, count) for j in range(1, count)])


def add_rows(sent):
    total, parts = sent
    for part in parts:
        total = total + part.astype(F32)
    return total


def send_both(partials, count):
    arrived = swap_core(jnp.concatenate([p[1].astype(BF16) for p in partials], axis=0))
    middle = partials[0][0].shape[0]
    sums = [
        (p[0] + part.astype(F32)).reshape(count, p[0].shape[0] // count, p[0].shape[1])
        for p, part in zip(partials, (arrived[:middle], arrived[middle:]))
    ]
    lows = [
        jnp.concatenate([part[j].astype(BF16) for part in sums], axis=0)
        for j in range(1, count)
    ]
    return ([part[0] for part in sums], [hop(lows[j - 1], j, count) for j in range(1, count)])


def by_place(me_ref, count, body):
    for number in range(count):
        pl.when(me_ref[0] == number)(functools.partial(body, number))


def pack_attn_kernel(count, me_ref, qkv_ref, proj_ref, *outs):
    columns = proj_ref.shape[2] // count

    def place(number):
        for j, out in enumerate(outs):
            at = (j ^ number) * columns
            for n in range(2):
                base = 4 * n * columns
                for k in range(3):
                    out[:, base + k * columns : base + (k + 1) * columns] = qkv_ref[
                        n, k, :, at : at + columns
                    ].astype(BF16)
                out[:, base + 3 * columns : base + 4 * columns] = proj_ref[
                    n, :, at : at + columns
                ].astype(BF16)

    by_place(me_ref, count, place)


def pack_attn(me, qkv, proj, count):
    slab, full = proj.shape[1:]
    shape = jax.ShapeDtypeStruct((slab, 8 * full // count), BF16)
    return pl.pallas_call(
        functools.partial(pack_attn_kernel, count),
        grid_spec=pltpu.PrefetchScalarGridSpec(
            num_scalar_prefetch=1,
            grid=(1,),
            in_specs=[
                pl.BlockSpec(qkv.shape, lambda i, m: (0, 0, 0, 0)),
                pl.BlockSpec(proj.shape, lambda i, m: (0, 0, 0)),
            ],
            out_specs=[pl.BlockSpec(shape.shape, lambda i, m: (0, 0))] * count,
        ),
        out_shape=[shape] * count,
    )(me, qkv, proj)


def pack_ff_kernel(count, me_ref, up_ref, down_ref, *outs):
    columns = up_ref.shape[1] // count

    def place(number):
        for j, out in enumerate(outs):
            at = (j ^ number) * columns
            out[:, :columns] = up_ref[:, at : at + columns].astype(BF16)
            out[:, columns:] = down_ref[:, at : at + columns].astype(BF16)

    by_place(me_ref, count, place)


def pack_ff(me, up, down, n, count):
    slab, full = up.shape[1:]
    shape = jax.ShapeDtypeStruct((slab, 2 * full // count), BF16)
    spec = pl.BlockSpec((None, slab, full), lambda i, m: (n, 0, 0))
    return pl.pallas_call(
        functools.partial(pack_ff_kernel, count),
        grid_spec=pltpu.PrefetchScalarGridSpec(
            num_scalar_prefetch=1,
            grid=(1,),
            in_specs=[spec, spec],
            out_specs=[pl.BlockSpec(shape.shape, lambda i, m: (0, 0))] * count,
        ),
        out_shape=[shape] * count,
    )(me, up, down)


def unpack_kernel(count, me_ref, *refs):
    blocks, out = (refs[:count], refs[count])
    slab = blocks[0].shape[0]

    def place(number):
        for j, block in enumerate(blocks):
            at = (j ^ number) * slab
            out[at : at + slab, :] = block[...]

    by_place(me_ref, count, place)


def unpack(me, blocks):
    count = len(blocks)
    slab, columns = blocks[0].shape
    return pl.pallas_call(
        functools.partial(unpack_kernel, count),
        grid_spec=pltpu.PrefetchScalarGridSpec(
            num_scalar_prefetch=1,
            grid=(1,),
            in_specs=[pl.BlockSpec((slab, columns), lambda i, m: (0, 0))] * count,
            out_specs=pl.BlockSpec((count * slab, columns), lambda i, m: (0, 0)),
        ),
        out_shape=jax.ShapeDtypeStruct((count * slab, columns), BF16),
    )(me, *blocks)


def merge_kernel(count, me_ref, own_ref, others_ref, out):
    slab = own_ref.shape[0]

    def place(number):
        for j in range(count):
            at = (j ^ number) * slab
            if j == 0:
                out[at : at + slab, :] = own_ref[...]
            else:
                out[at : at + slab, :] = others_ref[(j - 1) * slab : j * slab, :]

    by_place(me_ref, count, place)


def merge(me, own, others, slab, count):
    columns = own.shape[1]
    outer = own.shape[0] // slab
    return pl.pallas_call(
        functools.partial(merge_kernel, count),
        grid_spec=pltpu.PrefetchScalarGridSpec(
            num_scalar_prefetch=1,
            grid=(outer,),
            in_specs=[
                pl.BlockSpec((slab, columns), lambda i, m: (i, 0)),
                pl.BlockSpec(((count - 1) * slab, columns), lambda i, m: (i, 0)),
            ],
            out_specs=pl.BlockSpec((count * slab, columns), lambda i, m: (i, 0)),
        ),
        out_shape=jax.ShapeDtypeStruct((outer * count * slab, columns), BF16),
    )(me, own, others)


def adam_refs(gradient, weight, mean, second, outs):
    updated, mean_new, second_new = adam_step(weight, gradient, mean, second)
    for out, value in zip(outs, (gradient, updated, mean_new, second_new)):
        out[...] = value


def adam_ff_kernel(count, me_ref, *refs):
    blocks, (weight, mean, second) = (refs[:count], refs[count : count + 3])
    outs, gradient = (refs[-5:-1], refs[-1])
    wanted = pl.program_id(0) ^ me_ref[0]
    for j, block in enumerate(blocks):

        @pl.when(wanted == j)
        def take(block=block):
            gradient[...] = block[...].astype(F32)

    adam_refs(gradient[...], weight[...], mean[...], second[...], outs)


def adam_ff(me, blocks, half, weight, mean, second, n, before):
    count = len(blocks)
    slab, columns = (blocks[0].shape[0], blocks[0].shape[1] // 2)
    spec = pl.BlockSpec((None, slab, columns), lambda c, m: (n, 0, c))
    return pl.pallas_call(
        functools.partial(adam_ff_kernel, count),
        grid_spec=pltpu.PrefetchScalarGridSpec(
            num_scalar_prefetch=1,
            grid=(count,),
            in_specs=[pl.BlockSpec((slab, columns), lambda c, m: (0, half))] * count
            + [spec] * 3
            + [pl.BlockSpec(memory_space=pl.ANY)] * len(before),
            out_specs=[spec] * 4,
            scratch_shapes=[pltpu.VMEM((slab, columns), F32)],
        ),
        out_shape=[jax.ShapeDtypeStruct(weight.shape, F32)] * 4,
        input_output_aliases={1 + count + 3 + i: i for i in range(len(before))},
    )(me, *blocks, weight, mean, second, *before)


def adam_attn_kernel(count, parts, me_ref, *refs):
    blocks, (weight, mean, second) = (refs[:count], refs[count : count + 3])
    outs, gradient = (refs[-5:-1], refs[-1])
    columns = gradient.shape[1] // count
    step = pl.program_id(0)

    def place(number):
        for k in range(parts):

            @pl.when(step == k)
            def take(k=k):
                for j, block in enumerate(blocks):
                    at = (j ^ number) * columns
                    gradient[:, at : at + columns] = block[
                        :, k * columns : (k + 1) * columns
                    ].astype(F32)

    by_place(me_ref, count, place)
    adam_refs(gradient[...], weight[...], mean[...], second[...], outs)


def adam_attn(me, count, blocks, weight, mean, second):
    parts, slab, full = weight.shape
    size = blocks[0].shape[1] * len(blocks) // count
    places = [j if len(blocks) == 1 else 0 for j in range(count)]
    blocks = blocks * (count // len(blocks))
    spec = pl.BlockSpec((None, slab, full), lambda k, m: (k, 0, 0))
    return pl.pallas_call(
        functools.partial(adam_attn_kernel, count, parts),
        grid_spec=pltpu.PrefetchScalarGridSpec(
            num_scalar_prefetch=1,
            grid=(parts,),
            in_specs=[
                pl.BlockSpec((slab, size), functools.partial(lambda at, k, m: (0, at), at))
                for at in places
            ]
            + [spec] * 3,
            out_specs=[spec] * 4,
            scratch_shapes=[pltpu.VMEM((slab, full), F32)],
        ),
        out_shape=[jax.ShapeDtypeStruct(weight.shape, F32)] * 4,
    )(me, *blocks, weight, mean, second)


def exchange(blocks, count):
    return [blocks[0]] + [hop(blocks[j], j, count) for j in range(1, count)]


def after(values, *done):
    return jax.tree.map(lambda value: lax.optimization_barrier((value, done))[0], values)


def whole(array):
    return pl.BlockSpec(array.shape, lambda i, m: (0,) * len(array.shape))


def row_kernel(body, place, inputs, outputs, scratch=()):
    return pl.pallas_call(
        body,
        grid_spec=pltpu.PrefetchScalarGridSpec(
            num_scalar_prefetch=1,
            grid=(1,),
            in_specs=[whole(a) for a in inputs],
            out_specs=[whole(a) for a in outputs],
            scratch_shapes=list(scratch),
        ),
        out_shape=list(outputs),
    )(place, *inputs)


def fold(values):
    return jnp.sum(values.reshape(values.shape[0] // 8, 8, values.shape[1]), axis=0)


def arrived_rows(own, parts, where, offset):
    total = own[where, :]
    for part in parts:
        total = total + part[pl.ds(pl.multiple_of(offset, CHUNK), CHUNK), :].astype(F32)
    return total


def middle_back_kernel(n, me_ref, own, *refs):
    parts, (middle, attn, cotangent, mods) = (refs[:-7], refs[-7:-3])
    grad_out, low_out, sums_out = refs[-3:]
    zero = jnp.zeros((8, own.shape[1]), F32)
    scale, gate = (mods[n, 4:5, :], mods[n, 2:3, :])

    def step(i, sums):
        where = pl.ds(pl.multiple_of(i * CHUNK, CHUNK), CHUNK)
        grad = arrived_rows(own, parts, where, i * CHUNK)
        normed, inv_std = layer_norm(middle[where, :])
        total = cotangent[where, :].astype(F32) + norm_back(grad * (1.0 + scale), normed, inv_std)
        grad_out[where, :] = total
        low_out[where, :] = (total * gate).astype(BF16)
        terms = (total * attn[where, :], grad, grad * normed)
        return tuple(a + fold(b) for a, b in zip(sums, terms))

    sums = lax.fori_loop(0, own.shape[0] // CHUNK, step, (zero,) * 3)
    for k, value in enumerate(sums):
        sums_out[k : k + 1, :] = jnp.sum(value, axis=0, keepdims=True)


def middle_back(place, n, sent, middle, attn, cotangent, mods):
    own, parts = sent
    return row_kernel(
        functools.partial(middle_back_kernel, n),
        place,
        (own, *parts, middle, attn, cotangent, mods),
        (
            jax.ShapeDtypeStruct(own.shape, F32),
            jax.ShapeDtypeStruct(own.shape, BF16),
            jax.ShapeDtypeStruct((8, own.shape[1]), F32),
        ),
    )


def end_kernel(arrivals, me_ref, *refs):
    mods, back = (refs[0], refs[1 : 1 + arrivals])
    streams = refs[1 + arrivals : -4]
    each = len(streams) // 2
    grads_out, rows_out, owners_out, table = refs[-4:]
    offset = 0
    for n in range(2):
        own, tokens, grad_middle, cotangent, middle, sums, down = streams[n * each :][:7]
        parts = streams[n * each + 7 : (n + 1) * each]
        zero = jnp.zeros((8, own.shape[1]), F32)
        scale, gate = (mods[n, 1:2, :], mods[n, 5:6, :])

        def step(i, totals):
            where = pl.ds(pl.multiple_of(i * CHUNK, CHUNK), CHUNK)
            place = pl.ds(pl.multiple_of(offset + i * CHUNK, CHUNK), CHUNK)
            grad = arrived_rows(own, back, where, offset + i * CHUNK)
            normed, inv_std = layer_norm(tokens[where, :].astype(F32))
            grads_out[place, :] = grad_middle[where, :] + norm_back(
                grad * (1.0 + scale), normed, inv_std
            )
            total = arrived_rows(down, parts, where, i * CHUNK)
            rows_out[place, :] = middle[where, :] + gate * total
            terms = (grad, grad * normed, cotangent[where, :].astype(F32) * total)
            return tuple(a + fold(b) for a, b in zip(totals, terms))

        totals = lax.fori_loop(0, own.shape[0] // CHUNK, step, (zero,) * 3)
        for k, value in zip((0, 1, 5), totals):
            table[6 * n + k : 6 * n + k + 1, :] = jnp.sum(value, axis=0, keepdims=True)
        table[6 * n + 2 : 6 * n + 5, :] = sums[0:3, :]
        offset += own.shape[0]
    width = table.shape[1]
    devices, _, columns = owners_out.shape
    for n in range(2):
        for d in range(devices):
            done = 0
            while done < columns:
                k, at = divmod(d * columns + done, width)
                size = min(columns - done, width - at)
                owners_out[d, n : n + 1, done : done + size] = table[
                    6 * n + k : 6 * n + k + 1, at : at + size
                ]
                done += size


def end_rows(place, mods, sent_one, streams, down_sent, devices):
    owns, back = sent_one
    inputs = [mods, *back]
    for n in range(2):
        inputs += [owns[n], *streams[n], down_sent[n][0], *down_sent[n][1]]
    rows, width = back[0].shape
    columns = 6 * width // devices
    return row_kernel(
        functools.partial(end_kernel, len(back)),
        place,
        inputs,
        (
            jax.ShapeDtypeStruct((rows, width), F32),
            jax.ShapeDtypeStruct((rows, width), F32),
            jax.ShapeDtypeStruct((devices, 2, columns), F32),
        ),
        (pltpu.VMEM((16, width), F32),),
    )


def whole_rows_kernel(core_ref, own, other, *outs):
    for core in range(2):

        @pl.when(core_ref[0] == core)
        def place(core=core):
            start = 0
            for out in outs:
                length = out.shape[1]
                size = (own.shape[0] - start) if start else length // 2
                for number, source in ((core, own), (1 - core, other)):
                    count = min(size, length - number * size)
                    out[0, number * size : number * size + count, :] = source[
                        start : start + count, :
                    ]
                start += size


def whole_rows(core, own, lengths):
    return row_kernel(
        whole_rows_kernel,
        core,
        (own, swap_core(own)),
        [jax.ShapeDtypeStruct((1, length, own.shape[1]), F32) for length in lengths],
    )


def attn_gradient_kernel(columns, me_ref, *refs):
    shifted, grads, proj_ins, contexts = (refs[:2], refs[2:4], refs[4:6], refs[6:8])
    qkv_out, proj_out = refs[8:]
    full = grads[0].shape[1]
    split = columns // 256 * 256
    for low, high in ((0, split), (split, full)):
        total = None
        terms = list(zip(shifted, grads))
        if high > columns:
            terms += list(zip(proj_ins, contexts))
        for left, right in terms:
            part = dot_tn(left[...], right[:, low:high])
            total = part if total is None else total + part
        total = total.astype(BF16)
        if high > columns:
            qkv_out[:, low:] = total[:, : columns - low]
            proj_out[...] = total[:, columns - low :]
        else:
            qkv_out[:, low:high] = total


def attn_gradient(place, columns, shifted, grads, proj_ins, contexts):
    width = shifted[0].shape[1]
    full = grads[0].shape[1]
    tile = math.gcd(512, width)
    left = [pl.BlockSpec((a.shape[0], tile), lambda i, m: (0, i)) for a in shifted]
    right = [pl.BlockSpec(a.shape, lambda i, m: (0, 0)) for a in grads]
    rows = shifted[0].shape[0]
    return pl.pallas_call(
        functools.partial(attn_gradient_kernel, columns),
        grid_spec=pltpu.PrefetchScalarGridSpec(
            num_scalar_prefetch=1,
            grid=(width // tile,),
            in_specs=(left + right) * 2,
            out_specs=[
                pl.BlockSpec((tile, size), lambda i, m: (i, 0)) for size in (columns, full - columns)
            ],
        ),
        out_shape=[jax.ShapeDtypeStruct((width, size), BF16) for size in (columns, full - columns)],
        cost_estimate=pl.CostEstimate(
            flops=4 * rows * width * full, bytes_accessed=8 * rows * width, transcendentals=0
        ),
    )(place, *shifted, *grads, *proj_ins, *contexts)


def local(
    image_tokens,
    text_tokens,
    image_cotangent,
    text_cotangent,
    timesteps,
    mod_weight,
    mod_bias,
    qkv_weight,
    proj_weight,
    up_weight,
    down_weight,
    mean_mod,
    second_mod,
    mean_bias,
    second_bias,
    mean_qkv,
    second_qkv,
    mean_proj,
    second_proj,
    mean_up,
    second_up,
    mean_down,
    second_down,
):
    count = lax.axis_size("inner")
    cores = lax.axis_size("tensor")
    me = lax.axis_index("inner")
    core = lax.axis_index("tensor")
    every = ("outer", "inner", "tensor")
    streams = (0, 1)
    seq_count = timesteps.shape[0]
    devices = seq_count * cores
    column_count = mod_weight.shape[2]
    width = image_tokens.shape[2]
    slab = qkv_weight.shape[1]
    head_cols = qkv_weight.shape[3] // count
    heads = head_cols // HD
    unit_cols = up_weight.shape[2] // count
    lengths = (image_tokens.shape[1], text_tokens.shape[1])
    rows = tuple(-(-length // (16 * cores)) * 16 for length in lengths)

    place = me.astype(jnp.int32)[None]
    qkv_all = [a.transpose(0, 2, 1, 3) for a in (qkv_weight, mean_qkv, second_qkv)]
    proj_all = [a.transpose(0, 2, 1) for a in (proj_weight, mean_proj, second_proj)]
    up_all = (up_weight, mean_up, second_up)
    down_all = [a.transpose(0, 2, 1) for a in (down_weight, mean_down, second_down)]

    def full_weight(shard):
        return lax.all_gather(shard, "outer", axis=0, tiled=True)

    blocks = pack_attn(place, qkv_all[0], proj_all[0], count)
    own_full = full_weight(blocks[0])
    shard = jnp.concatenate(exchange(blocks, count)[1:], axis=0)
    attn_both = merge(place, own_full, full_weight(shard), slab, count)

    half_width = width // 2
    frequency = jnp.exp(-math.log(10000.0) * jnp.arange(half_width, dtype=F32) / half_width)
    angles = timesteps.astype(F32)[:, None] * frequency[None, :]
    all_cond = jax.nn.silu(jnp.concatenate([jnp.cos(angles), jnp.sin(angles)], axis=1)).astype(BF16)
    bias_low = lax.optimization_barrier(mod_bias.astype(BF16)).astype(F32)
    local_mod = (
        jnp.einsum("sd,ndc->snc", all_cond, mod_weight.astype(BF16), preferred_element_type=F32)
        + bias_low[None, :, :]
    )
    to_cores = jnp.broadcast_to(
        local_mod[:, None], (seq_count, cores, 2, column_count)
    ).reshape(devices, 2, column_count)
    spread = lax.all_to_all(to_cores, every, split_axis=0, concat_axis=0, tiled=True)
    mods = after(spread, shard).transpose(1, 0, 2).reshape(2, 6, width)

    def own_rows(tokens, size):
        short = cores * size - tokens.shape[1]
        padded = jnp.pad(tokens[0], ((0, short), (0, 0)))
        return lax.dynamic_slice(padded, (core * size, 0), (size, width))

    tokens = [own_rows(t, r) for t, r in zip((image_tokens, text_tokens), rows)]
    inputs = [t.astype(F32) for t in tokens]
    cotangents = [own_rows(t, r) for t, r in zip((image_cotangent, text_cotangent), rows)]
    valid = jnp.stack(
        [
            jnp.clip(lengths[1] - core * rows[1], 0, rows[1]),
            jnp.clip(lengths[1] - (1 - core) * rows[1], 0, rows[1]),
        ]
    ).astype(jnp.int32)

    shifted_one = []
    for n in streams:
        normed, _ = layer_norm(inputs[n])
        shifted_one.append((normed * (1.0 + mods[n, 1]) + mods[n, 0]).astype(BF16))
    shifted_one = finish_both(start_rows(jnp.concatenate(shifted_one, axis=0), count), rows[0])

    def ff_blocks(n, where):
        return exchange(pack_ff(where, up_all[0], down_all[0], n, count), count)

    shard = unpack(place, ff_blocks(0, after(place, shifted_one)))
    ff_full = [full_weight(shard)]
    blocks = ff_blocks(1, after(place, shard))
    gated = [
        (after(cotangents[n], shard).astype(F32) * mods[n, 5]).astype(BF16) for n in streams
    ]
    gated = start_rows(jnp.concatenate(gated, axis=0), count)

    wide = 4 * head_cols
    attn_full = [attn_both[:, :wide], attn_both[:, wide:]]
    qkv_pieces = [
        dot_nn(half, attn_full[n]).astype(BF16) for n in streams for half in shifted_one[n]
    ]
    *context_pieces, lse = attend(rows, heads, count, valid, qkv_pieces)
    contexts = (context_pieces[:2], context_pieces[2:])
    ff_full.append(full_weight(unpack(place, after(blocks, context_pieces))))
    attn_sums, middles, shifted_two, middle_rows = ([], [], [], [])
    for n in streams:
        partial = [dot_nt(half, attn_full[n]) for half in contexts[n]]
        attn_sum = add_rows(send_rows(partial[0], partial[1], count))
        middle = inputs[n] + mods[n, 2] * attn_sum
        normed, _ = layer_norm(middle)
        shifted = (normed * (1.0 + mods[n, 4]) + mods[n, 3]).astype(BF16)
        attn_sums.append(attn_sum)
        middles.append(middle)
        middle_rows.append(shifted)
        shifted_two.append(gather_rows(shifted, count))

    def outer_sum(gradient):
        return lax.psum_scatter(gradient, "outer", scatter_dimension=0, tiled=True)

    def owned(summed):
        return exchange(
            [
                lax.dynamic_slice(summed, ((me ^ j) * slab, 0), (slab, summed.shape[1]))
                for j in range(count)
            ],
            count,
        )

    down_ins = finish_both(after(gated, middle_rows[0]), rows[0])
    ff_full[0] = after(ff_full[0], middle_rows[0])
    grad_contexts, grad_middles, partial_rows, proj_ins = ([], [], [], [])
    ff_sums = []
    for n in streams:
        full = ff_full[n] if n == 0 else after(ff_full[n], proj_in, down_partials)
        up_full, down_full = (full[:, :unit_cols], full[:, unit_cols:])
        pairs = [gelu_pair(dot_nn(half, up_full)) for half in shifted_two[n]]
        hidden = [pair[0].astype(BF16) for pair in pairs]

        def down_gradient(where):
            total = dot_tn(where[0], hidden[0]) + dot_tn(where[1], hidden[1])
            return total.astype(BF16)

        grad_ins = down_ins[n]
        if n == 1:
            grad_down = down_gradient(grad_ins)
            grad_ins = after(grad_ins, grad_down)
        grad_pres = [
            (dot_nn(down_in, down_full) * pair[1]).astype(BF16)
            for down_in, pair in zip(grad_ins, pairs)
        ]
        partial = [dot_nt(grad_pre, up_full) for grad_pre in grad_pres]
        sent = send_rows(partial[0], partial[1], count)
        if n == 0:
            grad_down = down_gradient(after(grad_ins, partial))
            partial = (partial, grad_down)
        grad_pres = after(grad_pres, partial)
        total = dot_tn(shifted_two[n][0], grad_pres[0]) + dot_tn(shifted_two[n][1], grad_pres[1])
        grad_up = total.astype(BF16)
        ff_sums.append(outer_sum(jnp.concatenate([grad_down, grad_up], axis=1)))
        grad_middle, proj_in, sums = middle_back(
            place, n, after(sent, grad_up), middles[n], attn_sums[n], cotangents[n], mods
        )
        halves = gather_rows(proj_in, count)
        grad_contexts += [dot_nn(half, attn_full[n]).astype(BF16) for half in halves]
        proj_ins.append(halves)
        grad_middles.append(grad_middle)
        partial_rows.append(sums)
        if n == 0:
            down_partials = [dot_nt(half, down_full) for half in after(hidden, proj_in)]
    down_sent = send_rows(down_partials[0], down_partials[1], count)
    ff_sums[0] = after(ff_sums[0], grad_contexts)

    grad_pieces = attend_back(
        rows, heads, count, valid, qkv_pieces, context_pieces, grad_contexts, lse
    )
    grad_qkv_rows = (grad_pieces[:2], grad_pieces[2:])
    grad_attn = []
    for n in streams:
        grad_attn.append(
            attn_gradient(
                place, 3 * head_cols, shifted_one[n], grad_qkv_rows[n], proj_ins[n], contexts[n]
            )
        )
    qkv_sum = outer_sum(jnp.concatenate([pair[0] for pair in grad_attn], axis=1))
    proj_both = jnp.concatenate([pair[1] for pair in grad_attn], axis=1)
    proj_both = proj_both.reshape(-1, count, slab, proj_both.shape[1])
    grad_qkv_rows = after(grad_qkv_rows, grad_attn)
    partials = [[dot_nt(half, attn_full[n]) for half in grad_qkv_rows[n]] for n in streams]
    sent_one = send_both(partials, count)
    hidden, down_sent = after((hidden, down_sent), partials)
    down_partials = [dot_nt(half, down_full) for half in hidden]
    down_sent = [down_sent, send_rows(down_partials[0], down_partials[1], count)]

    def adam_both(n, before):
        blocks = owned(ff_sums[n])
        return [
            adam_ff(place, blocks, half, *arrays, n, outs)
            for half, arrays, outs in zip((0, 1), (down_all, up_all), before)
        ]

    ff_outs = adam_both(0, ((), ()))
    sent_one = after(sent_one, down_partials, ff_outs[0][0], ff_outs[1][0])
    ff_sums[1] = after(ff_sums[1], sent_one[1], [sent[1] for sent in down_sent])
    grad_rows, out_rows, to_owners = end_rows(
        place,
        mods,
        sent_one,
        [(tokens[n], grad_middles[n], cotangents[n], middles[n], partial_rows[n]) for n in streams],
        down_sent,
        devices,
    )

    blocks = exchange(
        [
            lax.dynamic_index_in_dim(proj_both, me ^ j, axis=1, keepdims=False)
            for j in range(count)
        ],
        count,
    )
    blocks = after(blocks, to_owners)
    proj_sum = outer_sum(jnp.concatenate(blocks, axis=2).reshape(-1, count * proj_both.shape[3]))

    received = lax.all_to_all(to_owners, every, split_axis=0, concat_axis=0, tiled=True)
    ff_outs = adam_both(1, ff_outs)
    received = after(received, ff_outs[0][0], ff_outs[1][0])
    own_columns = received.reshape(seq_count, cores, 2, column_count).sum(axis=1)
    grad_mod = jnp.einsum(
        "sd,snc->ndc", all_cond.astype(F32), own_columns, precision=lax.Precision.HIGHEST
    )
    grad_bias = jnp.sum(own_columns, axis=0)
    new_mod, mean_mod_next, second_mod_next = adam_step(mod_weight, grad_mod, mean_mod, second_mod)
    new_bias, mean_bias_next, second_bias_next = adam_step(
        mod_bias, grad_bias, mean_bias, second_bias
    )

    core_place = core.astype(jnp.int32)[None]
    image_out, text_out = whole_rows(core_place, out_rows, lengths)
    image_grad, text_grad = whole_rows(core_place, grad_rows, lengths)

    down_outs, up_outs = ff_outs
    qkv_outs = adam_attn(
        place,
        count,
        owned(after(qkv_sum, new_mod, text_out, text_grad)),
        *(a.reshape(6, *a.shape[2:]) for a in qkv_all),
    )
    proj_outs = adam_attn(
        place, count, [after(proj_sum, qkv_outs[0], up_outs[0], down_outs[0])], *proj_all
    )
    grad_up, new_up, mean_up_next, second_up_next = up_outs
    grad_down, new_down, mean_down_next, second_down_next = (
        a.transpose(0, 2, 1) for a in down_outs
    )
    grad_qkv, new_qkv, mean_qkv_next, second_qkv_next = (
        a.reshape(qkv_all[0].shape).transpose(0, 2, 1, 3) for a in qkv_outs
    )
    grad_proj, new_proj, mean_proj_next, second_proj_next = (
        a.transpose(0, 2, 1) for a in proj_outs
    )
    return (
        image_out,
        text_out,
        image_grad,
        text_grad,
        grad_mod,
        grad_bias,
        grad_qkv,
        grad_proj,
        grad_up,
        grad_down,
        new_mod,
        new_bias,
        new_qkv,
        new_proj,
        new_up,
        new_down,
        mean_mod_next,
        second_mod_next,
        mean_bias_next,
        second_bias_next,
        mean_qkv_next,
        second_qkv_next,
        mean_proj_next,
        second_proj_next,
        mean_up_next,
        second_up_next,
        mean_down_next,
        second_down_next,
    )


def solution(mesh):
    dp, cores = mesh.devices.shape
    inner = math.gcd(dp, INNER)
    split = Mesh(mesh.devices.reshape(dp // inner, inner, cores), ("outer", "inner", "tensor"))
    group = ("outer", "inner")
    every = ("outer", "inner", "tensor")
    tokens = P(group, None, None)
    mod, bias = (P(None, None, every), P(None, every))
    qkv = P(None, group, None, "tensor")
    columns = P(None, group, "tensor")
    rows = P(None, "tensor", group)
    return jax.shard_map(
        local,
        mesh=split,
        in_specs=(tokens,) * 4
        + (P(),)
        + (mod, bias, qkv, rows, columns, rows)
        + (mod, mod, bias, bias, qkv, qkv, rows, rows, columns, columns, rows, rows),
        out_specs=(tokens,) * 4
        + (mod, bias, qkv, rows, columns, rows)
        + (mod, bias, qkv, rows, columns, rows)
        + (mod, mod, bias, bias, qkv, qkv, rows, rows, columns, columns, rows, rows),
        check_vma=False,
    )
```
